128 devices in a mesh: col: 16 (over y, z_lo, core), row: 8 (over z_hi, x).
Axes of the slice: x: 4, y: 4, z: 4 (z_hi: 2, z_lo: 2; z = z_hi * 2 + z_lo), core: 2. Of those that a mesh axis runs over, the one named last changes fastest.
Arguments:
- valence: float32 [32, 64, 4096], P('row'), may hold values from -6 to 6
- conduction: float32 [64, 64, 4096], P('col'), may hold values from -6 to 6
- valence_energy: float32 [32], P('row'), may hold values from -10 to -0.5
- conduction_energy: float32 [64], P('col'), may hold values from 0.5 to 10
- pair_list: int32 [1024, 2], P(('col', 'row')), may hold values from 0 to 63, as said below
- sphere_index: int32 [16384], replicated, may hold values from 0 to 262143, as said below
Outputs:
- response: float32 [16384, 16384], P('row', 'col')
The draws below stay inside these ranges and needn't reach their ends.
Inputs may be any that keep to these rules, and one draw needn't show every extreme that they name: `pair_list`: the 8 rows of the device with col index c and row index r (the block of rows that starts at (c * 8 + r) * 8) are distinct pairs, with valence index from r * 4 to (r + 1) * 4 - 1 and conduction index from c * 4 to (c + 1) * 4 - 1. `sphere_index`: distinct flat indices a * 64**2 + b * 64 + c of grid points.
All inputs are finite; a program needn't handle non-finite values.
Results may differ from the reference program's by a relative error of at most 0.004.
Values may be sent and summed in bfloat16 or wider, within the bound.
No kernel may reach another device: no remote copies, remote signals or barrier semaphores. Data moves between devices by JAX's collectives and lax.ppermute only.
A program may use at most 192 MiB of HBM per device.

```python
import jax
import jax.numpy as jnp
from jax import lax

G1 = 64
NG = 16384
PAIR_DEV = 8
VAL_DEV = 4
CON_DEV = 4
NV = 32
NC = 64
PAIRS = 1024


def draw_pair_list(key, part):
    combos = VAL_DEV * CON_DEV
    blocks = PAIRS // PAIR_DEV
    row_count = NV // VAL_DEV

    def one_block(block):
        block_key = jax.random.fold_in(key, block)
        first_val = jax.random.randint(jax.random.fold_in(block_key, 11), (), 0, VAL_DEV).astype(jnp.int32)
        second_val = jax.random.randint(jax.random.fold_in(block_key, 13), (), 0, VAL_DEV).astype(jnp.int32)
        first_pick = first_val * CON_DEV
        second_pick = second_val * CON_DEV + CON_DEV - 1
        ranks = jax.random.permutation(jax.random.fold_in(block_key, 17), combos).astype(jnp.int32)
        every = jnp.arange(combos, dtype=jnp.int32)
        ranks = jnp.where(every == first_pick, -2, ranks)
        ranks = jnp.where(every == second_pick, -1, ranks)
        picks = jnp.argsort(ranks, stable=True).astype(jnp.int32)[:PAIR_DEV]
        order = jax.random.permutation(jax.random.fold_in(block_key, 7), PAIR_DEV)
        picks = picks[order]
        col_index = block // row_count
        row_index = block % row_count
        valence_pick = row_index * VAL_DEV + picks // CON_DEV
        conduction_pick = col_index * CON_DEV + picks % CON_DEV
        return jnp.stack([valence_pick, conduction_pick], axis=1)
    return jax.vmap(one_block)(jnp.arange(blocks, dtype=jnp.int32)).reshape(PAIRS, 2).astype(jnp.int32)


def draw_sphere_index(key, part):
    points = G1 ** 3
    inner = jax.random.permutation(key, points - 2)[:NG - 2].astype(jnp.int32) + 1
    values = jnp.concatenate([jnp.array([0, points - 1], jnp.int32), inner])
    order = jax.random.permutation(jax.random.fold_in(key, 3), NG)
    return values[order].astype(jnp.int32)


def shard_levels(stream_key, shape, shards, least, high):
    def one(axis_at, parts):
        draws = jax.random.uniform(jax.random.fold_in(jax.random.fold_in(stream_key, 6), axis_at), (parts,), jnp.float32, least / len(shards), high / len(shards))
        return jnp.repeat(jnp.exp(draws), shape[axis_at] // parts).reshape((-1,) + (1,) * (len(shape) - axis_at - 1))

    factor_of = one(*shards[0])
    for cut in shards[1:]:
        factor_of = factor_of * one(*cut)
    return factor_of


def noise(own_key, extent, deviation, reach, shards=(), kind=jnp.bfloat16):
    values = jax.random.normal(own_key, extent, jnp.float32) * deviation
    if len(shards) > 0:
        values = shard_levels(own_key, extent, shards, -0.22, 0.18) * values
    return jnp.clip(values, min=-reach, max=reach).astype(kind)


def setup_inputs(seed: int = 0) -> dict:
    seeds = jax.random.split(jax.random.key(seed), 7)
    valence = noise(seeds[0], (NV, G1, G1 * G1), 1.0, 6.0, ((0, 8),), jnp.float32)
    conduction = noise(seeds[1], (NC, G1, G1 * G1), 1.0, 6.0, ((0, 16),), jnp.float32)
    valence_energy = jnp.clip(-10.0 + 9.5 * jax.random.uniform(seeds[2], (NV,), jnp.float32) ** shard_levels(seeds[2], (NV,), ((0, 8),), -0.2, 0.2), -10.0, -0.5)
    conduction_energy = jnp.clip(0.5 + 9.5 * jax.random.uniform(seeds[3], (NC,), jnp.float32) ** shard_levels(seeds[3], (NC,), ((0, 16),), -0.2, 0.2), 0.5, 10.0)
    pair_list = draw_pair_list(jax.random.fold_in(seeds[6], 71), 0)
    sphere_index = draw_sphere_index(jax.random.fold_in(seeds[6], 71), 0)
    return {"valence": valence, "conduction": conduction, "valence_energy": valence_energy, "conduction_energy": conduction_energy, "pair_list": pair_list, "sphere_index": sphere_index}


def pair_density(valence, conduction, sphere_index, entry):
    grid_edge = valence.shape[1]
    product = (valence[entry[0]] * conduction[entry[1]]).reshape(grid_edge, grid_edge, grid_edge)
    spectrum = jnp.fft.fftn(product).reshape(-1)[sphere_index]
    scale = grid_edge ** -1.5
    return jnp.stack([jnp.real(spectrum), jnp.imag(spectrum)]) * scale


def reference(valence, conduction, valence_energy, conduction_energy, pair_list, sphere_index):
    density = lax.map(lambda entry: pair_density(valence, conduction, sphere_index, entry), pair_list)
    energy_gap = conduction_energy[pair_list[:, 1]] - valence_energy[pair_list[:, 0]]
    weight = -4.0 / (PAIRS * energy_gap)
    weighted = (weight[:, None, None] * density).astype(jnp.bfloat16)
    unweighted = density.astype(jnp.bfloat16)
    return jnp.dot(weighted.reshape(2 * PAIRS, NG).T, unweighted.reshape(2 * PAIRS, NG), preferred_element_type=jnp.float32)
```

```python
import math

import jax
import jax.numpy as jnp
import numpy as np
from jax import lax
from jax.experimental import pallas as pl
from jax.experimental.pallas import tpu as pltpu
from jax.sharding import PartitionSpec as P

EDGE = 64
HALF = EDGE // 2
LANES = 128
BF = jnp.bfloat16
F32 = jnp.float32


def two_terms(table):
    high = table.astype(np.float32).astype(BF)
    low = (table - high.astype(np.float64)).astype(BF)
    return np.asarray(high), np.asarray(low)


def x_table():
    x = np.arange(EDGE)
    a = np.arange(HALF)
    angle = 2.0 * np.pi * ((a[:, None] * x[None, :]) % EDGE) / EDGE
    table = np.concatenate([np.cos(angle), -np.sin(angle)], axis=0)
    table[HALF] = 1.0 - 2.0 * (x % 2)
    high, low = two_terms(table)
    return np.concatenate([high, high, low], axis=1)


def z_table():
    z = np.arange(EDGE)
    angle = 2.0 * np.pi * ((z[:, None] * z[None, :]) % EDGE) / EDGE
    cosine, sine = np.cos(angle), np.sin(angle)
    table = np.block([[cosine, -sine], [sine, cosine]]) * EDGE ** (-1.5)
    high, low = two_terms(table)
    return np.block([[high, low], [high, np.zeros_like(low)]]).astype(BF)


def y_table():
    angle = 2.0 * np.pi * np.arange(HALF) / EDGE
    odd = np.arange(LANES)[None, :] >= EDGE
    real = np.where(odd, np.cos(angle)[:, None], 1.0)
    imag = np.where(odd, -np.sin(angle)[:, None], 0.0)
    return np.concatenate([real, imag], axis=0).astype(np.float32)


def small_dft(re, im):
    n = len(re)
    if n == 1:
        return re, im
    even_re, even_im = small_dft(re[0::2], im[0::2])
    odd_re, odd_im = small_dft(re[1::2], im[1::2])
    out_re, out_im = [None] * n, [None] * n
    for k in range(n // 2):
        r, i = odd_re[k], odd_im[k]
        if k == 0:
            pass
        elif 4 * k == n:
            r, i = i, -r
        elif 8 * k == n:
            s = math.sqrt(0.5)
            r, i = (r + i) * s, (i - r) * s
        elif 8 * k == 3 * n:
            s = math.sqrt(0.5)
            r, i = (i - r) * s, (r + i) * -s
        else:
            c, s = math.cos(2 * math.pi * k / n), math.sin(2 * math.pi * k / n)
            r, i = r * c + i * s, i * c - r * s
        out_re[k], out_im[k] = even_re[k] + r, even_im[k] + i
        out_re[k + n // 2], out_im[k + n // 2] = even_re[k] - r, even_im[k] - i
    return out_re, out_im


def split(value):
    high = value.astype(BF)
    return high, (value - high.astype(F32)).astype(BF)


def density_kernel(
    pairs,
    lines,
    valence,
    conduction,
    weight,
    point,
    wave,
    x_factors,
    z_factors,
    y_factors,
    left,
    right,
    staged,
    table,
):
    n_pairs = 8
    wide = 2 * LANES

    def x_stage(chunk, carry):
        lanes = pl.ds(pl.multiple_of(chunk * wide, wide), wide)
        for p in range(n_pairs):
            product = valence[pairs[2 * p], :, lanes] * conduction[pairs[2 * p + 1], :, lanes]
            high, low = split(product)
            spectrum = jnp.dot(
                x_factors[...],
                jnp.concatenate([high, low, high], axis=0),
                preferred_element_type=F32,
            )
            for h in range(2):
                staged[2 * chunk + h, pl.ds(p * EDGE, EDGE), :] = spectrum[:, h * LANES : (h + 1) * LANES]
        return carry

    lax.fori_loop(0, EDGE * EDGE // wide, x_stage, 0)

    first = lax.broadcasted_iota(jnp.int32, (8, LANES), 1) < EDGE

    def yz_stage(a, carry):
        re = [staged[y, pl.ds(a, 8, stride=EDGE), :] for y in range(HALF)]
        im = [staged[y, pl.ds(a + HALF, 8, stride=EDGE), :] for y in range(HALF)]
        re, im = small_dft(re, im)
        lower, upper = [], []
        for b in range(HALF):
            r, i = re[b], im[b]
            if b:
                c = y_factors[pl.ds(b, 8, stride=0), :]
                s = y_factors[pl.ds(b + HALF, 8, stride=0), :]
                r, i = r * c - i * s, r * s + i * c
            even = jnp.where(first, r, pltpu.roll(i, EDGE, 1))
            odd = jnp.where(first, pltpu.roll(r, EDGE, 1), i)
            lower.append(even + odd)
            upper.append(even - odd)
        high, low = split(jnp.concatenate(lower + upper, axis=0))
        out = jnp.dot(
            jnp.concatenate([high, low], axis=1), z_factors[...], preferred_element_type=F32
        )
        out = out[:, :LANES] + out[:, LANES:]
        table[pl.ds(a * EDGE, EDGE)] = out.reshape(EDGE, 8, LANES)
        return carry

    lax.fori_loop(0, HALF, yz_stage, 0)

    lane = lax.broadcasted_iota(jnp.int32, (8, LANES), 1)
    mirror = (lane & EDGE) | ((EDGE - lane) & (EDGE - 1))

    def one_line(b):
        return table[b], jnp.take_along_axis(table[(EDGE - b) & (EDGE - 1)], mirror, axis=1)

    def store_line(b, here, there):
        total, delta = 0.5 * (here + there), 0.5 * (here - there)
        swapped_total, swapped_delta = pltpu.roll(total, EDGE, 1), pltpu.roll(delta, EDGE, 1)
        table[b] = jnp.where(first, total, delta)
        table[HALF * EDGE + b] = jnp.where(first, swapped_total, -swapped_delta)

    for b in range(HALF + 1):
        mine = one_line(b)
        other = (EDGE - b) & (EDGE - 1)
        if other != b:
            theirs = one_line(other)
            store_line(other, *theirs)
        store_line(b, *mine)

    per_row, per_col = left.shape[2] // LANES, right.shape[2] // LANES
    slot = lane & (EDGE - 1)
    w = weight[...]

    def select(q, carry):
        parts = []
        for h in range(2):
            index = point[pl.ds(2 * q + h, 8, stride=0), :]
            c = jnp.where(index >= (HALF + 1) * EDGE * EDGE, EDGE - index, index) & (EDGE - 1)
            take = c + jnp.where(first, h * EDGE, EDGE - h * EDGE)
            picked = jnp.zeros((8, LANES), F32)
            for j in range(EDGE):
                tile = table[lines[q * LANES + h * EDGE + j]]
                picked = jnp.where(slot == j, jnp.take_along_axis(tile, take, axis=1), picked)
            parts.append(picked)
        re = jnp.where(first, parts[0], parts[1])
        im = pltpu.roll(jnp.where(first, parts[1], parts[0]), EDGE, 1)
        index = wave[pl.ds(q, 8, stride=0), :]
        im = jnp.where(index >= (HALF + 1) * EDGE * EDGE, -im, im)
        plain = jnp.concatenate([re, im], axis=0).astype(BF)
        scaled = jnp.concatenate([w * re, w * im], axis=0).astype(BF)
        at = pl.multiple_of((q % per_row) * LANES, LANES)
        left[q // per_row, :, pl.ds(at, LANES)] = scaled
        at = pl.multiple_of((q % per_col) * LANES, LANES)
        right[q // per_col, :, pl.ds(at, LANES)] = plain
        return carry

    lax.fori_loop(0, wave.shape[0], select, 0)


def densities(n_row, n_col, valence, conduction, valence_energy, conduction_energy, pair_list, sphere_index):
    n_pairs, waves = pair_list.shape[0], sphere_index.shape[0]
    total_pairs = n_pairs * n_row * n_col
    v = pair_list[:, 0] - lax.axis_index("row") * valence.shape[0]
    c = pair_list[:, 1] - lax.axis_index("col") * conduction.shape[0]
    v_hot = v[:, None] == jnp.arange(valence.shape[0])[None, :]
    c_hot = c[:, None] == jnp.arange(conduction.shape[0])[None, :]
    gap = jnp.sum(jnp.where(c_hot, conduction_energy[None, :], 0.0), axis=1) - jnp.sum(
        jnp.where(v_hot, valence_energy[None, :], 0.0), axis=1
    )
    weight = jnp.broadcast_to((-4.0 / (total_pairs * gap))[:, None], (n_pairs, LANES))
    mirrored = sphere_index >= (HALF + 1) * EDGE * EDGE
    a, b = sphere_index // (EDGE * EDGE), (sphere_index // EDGE) % EDGE
    a = jnp.where(mirrored, EDGE - a, a)
    b = jnp.where(mirrored, (EDGE - b) % EDGE, b)
    lines = a * EDGE + b
    halves = sphere_index.reshape(-1, EDGE)
    smem = pl.BlockSpec(memory_space=pltpu.SMEM)
    vmem = pl.BlockSpec(memory_space=pltpu.VMEM)
    return pl.pallas_call(
        density_kernel,
        in_specs=[smem, smem] + [vmem] * 8,
        out_specs=[vmem, vmem],
        out_shape=[
            jax.ShapeDtypeStruct((n_row, 2 * n_pairs, waves // n_row), BF),
            jax.ShapeDtypeStruct((n_col, 2 * n_pairs, waves // n_col), BF),
        ],
        scratch_shapes=[
            pltpu.VMEM((HALF, n_pairs * EDGE, LANES), F32),
            pltpu.VMEM(((HALF + 1) * EDGE, 8, LANES), F32),
        ],
        compiler_params=pltpu.CompilerParams(vmem_limit_bytes=48 * 1024 * 1024),
        name="density",
    )(
        jnp.stack([v, c], axis=1).reshape(-1),
        lines,
        valence,
        conduction,
        weight,
        jnp.concatenate([halves, halves], axis=1),
        sphere_index.reshape(-1, LANES),
        jnp.asarray(x_table()),
        jnp.asarray(z_table()),
        jnp.asarray(y_table()),
    )


def per_device(valence, conduction, valence_energy, conduction_energy, pair_list, sphere_index):
    n_row, n_col = lax.axis_size("row"), lax.axis_size("col")
    left, right = densities(
        n_row, n_col, valence, conduction, valence_energy, conduction_energy, pair_list, sphere_index
    )
    left = lax.all_to_all(left, "row", split_axis=0, concat_axis=0, tiled=True)
    right = lax.all_to_all(right, "col", split_axis=0, concat_axis=0, tiled=True)
    left = lax.all_gather(left, "col", axis=0, tiled=False)
    right = lax.all_gather(right, "row", axis=0, tiled=False)
    return jnp.einsum("crkg,rckh->gh", left, right, preferred_element_type=F32)


def solution(mesh):
    return jax.shard_map(
        per_device,
        mesh=mesh,
        in_specs=(
            P("row", None, None),
            P("col", None, None),
            P("row"),
            P("col"),
            P(("col", "row"), None),
            P(),
        ),
        out_specs=P("row", "col"),
        check_vma=False,
    )
```

```python
import math

import jax
import jax.numpy as jnp
import numpy as np
from jax import lax
from jax.experimental import pallas as pl
from jax.experimental.pallas import tpu as pltpu
from jax.sharding import PartitionSpec as P

EDGE = 64
HALF = EDGE // 2
LANES = 128
BF = jnp.bfloat16
F32 = jnp.float32


def two_terms(table):
    high = table.astype(np.float32).astype(BF)
    low = (table - high.astype(np.float64)).astype(BF)
    return np.asarray(high), np.asarray(low)


def x_table():
    x = np.arange(EDGE)
    a = np.arange(HALF)
    angle = 2.0 * np.pi * ((a[:, None] * x[None, :]) % EDGE) / EDGE
    table = np.concatenate([np.cos(angle), -np.sin(angle)], axis=0)
    table[HALF] = 1.0 - 2.0 * (x % 2)
    high, low = two_terms(table)
    return np.concatenate([high, high, low], axis=1)


def z_table():
    z = np.arange(EDGE)
    angle = 2.0 * np.pi * ((z[:, None] * z[None, :]) % EDGE) / EDGE
    cosine, sine = np.cos(angle), np.sin(angle)
    table = np.block([[cosine, -sine], [sine, cosine]]) * EDGE ** (-1.5)
    high, low = two_terms(table)
    return np.block([[high, low], [high, np.zeros_like(low)]]).astype(BF)


def y_table():
    angle = 2.0 * np.pi * np.arange(HALF) / EDGE
    odd = np.arange(LANES)[None, :] >= EDGE
    real = np.where(odd, np.cos(angle)[:, None], 1.0)
    imag = np.where(odd, -np.sin(angle)[:, None], 0.0)
    return np.concatenate([real, imag], axis=0).astype(np.float32)


def small_dft(re, im):
    n = len(re)
    if n == 1:
        return re, im
    even_re, even_im = small_dft(re[0::2], im[0::2])
    odd_re, odd_im = small_dft(re[1::2], im[1::2])
    out_re, out_im = [None] * n, [None] * n
    for k in range(n // 2):
        r, i = odd_re[k], odd_im[k]
        if k == 0:
            pass
        elif 4 * k == n:
            r, i = i, -r
        elif 8 * k == n:
            s = math.sqrt(0.5)
            r, i = (r + i) * s, (i - r) * s
        elif 8 * k == 3 * n:
            s = math.sqrt(0.5)
            r, i = (i - r) * s, (r + i) * -s
        else:
            c, s = math.cos(2 * math.pi * k / n), math.sin(2 * math.pi * k / n)
            r, i = r * c + i * s, i * c - r * s
        out_re[k], out_im[k] = even_re[k] + r, even_im[k] + i
        out_re[k + n // 2], out_im[k + n // 2] = even_re[k] - r, even_im[k] - i
    return out_re, out_im


def split(value):
    high = value.astype(BF)
    return high, (value - high.astype(F32)).astype(BF)


def density_kernel(
    pairs,
    lines,
    valence,
    conduction,
    weight,
    point,
    wave,
    x_factors,
    z_factors,
    y_factors,
    left,
    right,
    staged,
    table,
):
    n_pairs = 8
    wide = 2 * LANES

    def x_stage(chunk, carry):
        lanes = pl.ds(pl.multiple_of(chunk * wide, wide), wide)
        for p in range(n_pairs):
            product = valence[pairs[2 * p], :, lanes] * conduction[pairs[2 * p + 1], :, lanes]
            high, low = split(product)
            spectrum = jnp.dot(
                x_factors[...],
                jnp.concatenate([high, low, high], axis=0),
                preferred_element_type=F32,
            )
            for h in range(2):
                staged[2 * chunk + h, pl.ds(p, EDGE, stride=8), :] = spectrum[:, h * LANES : (h + 1) * LANES]
        return carry

    lax.fori_loop(0, EDGE * EDGE // wide, x_stage, 0)

    first = lax.broadcasted_iota(jnp.int32, (8, LANES), 1) < EDGE

    def yz_stage(a, carry):
        re = [staged[y, pl.ds(pl.multiple_of(a * 8, 8), 8), :] for y in range(HALF)]
        im = [staged[y, pl.ds(pl.multiple_of((a + HALF) * 8, 8), 8), :] for y in range(HALF)]
        re, im = small_dft(re, im)
        lower, upper = [], []
        for b in range(HALF):
            r, i = re[b], im[b]
            if b:
                c = y_factors[pl.ds(b, 8, stride=0), :]
                s = y_factors[pl.ds(b + HALF, 8, stride=0), :]
                r, i = r * c - i * s, r * s + i * c
            even = jnp.where(first, r, pltpu.roll(i, EDGE, 1))
            odd = jnp.where(first, pltpu.roll(r, EDGE, 1), i)
            lower.append(even + odd)
            upper.append(even - odd)
        high, low = split(jnp.concatenate(lower + upper, axis=0))
        out = jnp.dot(
            jnp.concatenate([high, low], axis=1), z_factors[...], preferred_element_type=F32
        )
        out = out[:, :LANES] + out[:, LANES:]
        table[pl.ds(a * EDGE, EDGE)] = out.reshape(EDGE, 8, LANES)
        return carry

    lax.fori_loop(0, HALF, yz_stage, 0)

    lane = lax.broadcasted_iota(jnp.int32, (8, LANES), 1)
    mirror = (lane & EDGE) | ((EDGE - lane) & (EDGE - 1))

    def one_line(b):
        return table[b], jnp.take_along_axis(table[(EDGE - b) & (EDGE - 1)], mirror, axis=1)

    def store_line(b, here, there):
        total, delta = 0.5 * (here + there), 0.5 * (here - there)
        swapped_total, swapped_delta = pltpu.roll(total, EDGE, 1), pltpu.roll(delta, EDGE, 1)
        table[b] = jnp.where(first, total, delta)
        table[HALF * EDGE + b] = jnp.where(first, swapped_total, -swapped_delta)

    for b in range(HALF + 1):
        mine = one_line(b)
        other = (EDGE - b) & (EDGE - 1)
        if other != b:
            theirs = one_line(other)
            store_line(other, *theirs)
        store_line(b, *mine)

    per_row, per_col = left.shape[2] // LANES, right.shape[2] // LANES
    slot = lane & (EDGE - 1)
    w = weight[...]
    bits = [(slot & (1 << i)) != 0 for i in range(6)]

    def select(q, carry):
        parts = []
        for h in range(2):
            index = point[pl.ds(2 * q + h, 8, stride=0), :]
            c = jnp.where(index >= (HALF + 1) * EDGE * EDGE, EDGE - index, index) & (EDGE - 1)
            take = c + jnp.where(first, h * EDGE, EDGE - h * EDGE)
            def merge(level, j):
                if level < 0:
                    tile = table[lines[q * LANES + h * EDGE + j]]
                    return jnp.take_along_axis(tile, take, axis=1)
                one = merge(level - 1, j)
                other = merge(level - 1, j + (1 << level))
                return jnp.where(bits[level], other, one)

            picked = merge(5, 0)
            parts.append(picked)
        re = jnp.where(first, parts[0], parts[1])
        im = pltpu.roll(jnp.where(first, parts[1], parts[0]), EDGE, 1)
        index = wave[pl.ds(q, 8, stride=0), :]
        im = jnp.where(index >= (HALF + 1) * EDGE * EDGE, -im, im)
        plain = jnp.concatenate([re, im], axis=0).astype(BF)
        scaled = jnp.concatenate([w * re, w * im], axis=0).astype(BF)
        at = pl.multiple_of((q % per_row) * LANES, LANES)
        left[q // per_row, :, pl.ds(at, LANES)] = scaled
        at = pl.multiple_of((q % per_col) * LANES, LANES)
        right[q // per_col, :, pl.ds(at, LANES)] = plain
        return carry

    lax.fori_loop(0, wave.shape[0], select, 0, unroll=4)


def densities(n_row, n_col, valence, conduction, valence_energy, conduction_energy, pair_list, sphere_index):
    n_pairs, waves = pair_list.shape[0], sphere_index.shape[0]
    total_pairs = n_pairs * n_row * n_col
    v = pair_list[:, 0] - lax.axis_index("row") * valence.shape[0]
    c = pair_list[:, 1] - lax.axis_index("col") * conduction.shape[0]
    v_hot = v[:, None] == jnp.arange(valence.shape[0])[None, :]
    c_hot = c[:, None] == jnp.arange(conduction.shape[0])[None, :]
    gap = jnp.sum(jnp.where(c_hot, conduction_energy[None, :], 0.0), axis=1) - jnp.sum(
        jnp.where(v_hot, valence_energy[None, :], 0.0), axis=1
    )
    weight = jnp.broadcast_to((-4.0 / (total_pairs * gap))[:, None], (n_pairs, LANES))
    mirrored = sphere_index >= (HALF + 1) * EDGE * EDGE
    a, b = sphere_index // (EDGE * EDGE), (sphere_index // EDGE) % EDGE
    a = jnp.where(mirrored, EDGE - a, a)
    b = jnp.where(mirrored, (EDGE - b) % EDGE, b)
    lines = a * EDGE + b
    halves = sphere_index.reshape(-1, EDGE)
    smem = pl.BlockSpec(memory_space=pltpu.SMEM)
    vmem = pl.BlockSpec(memory_space=pltpu.VMEM)
    return pl.pallas_call(
        density_kernel,
        in_specs=[smem, smem] + [vmem] * 8,
        out_specs=[vmem, vmem],
        out_shape=[
            jax.ShapeDtypeStruct((n_row, 2 * n_pairs, waves // n_row), BF),
            jax.ShapeDtypeStruct((n_col, 2 * n_pairs, waves // n_col), BF),
        ],
        scratch_shapes=[
            pltpu.VMEM((HALF, n_pairs * EDGE, LANES), F32),
            pltpu.VMEM(((HALF + 1) * EDGE, 8, LANES), F32),
        ],
        compiler_params=pltpu.CompilerParams(vmem_limit_bytes=48 * 1024 * 1024),
        name="density",
    )(
        jnp.stack([v, c], axis=1).reshape(-1),
        lines,
        valence,
        conduction,
        weight,
        jnp.concatenate([halves, halves], axis=1),
        sphere_index.reshape(-1, LANES),
        jnp.asarray(x_table()),
        jnp.asarray(z_table()),
        jnp.asarray(y_table()),
    )


def product_kernel(n_left, n_right, left_slots, right_slots, *refs):
    left_in, right_in = refs[:n_left], refs[n_left : n_left + n_right]
    out, left, right, left_sem, right_sem = refs[n_left + n_right :]

    @pl.when(pl.program_id(0) == 0)
    def _():
        copies = [
            pltpu.make_async_copy(piece, right.at[:, right_slots[j]], right_sem.at[j])
            for j, piece in enumerate(right_in)
        ] + [
            pltpu.make_async_copy(piece, left.at[left_slots[i]], left_sem.at[i])
            for i, piece in enumerate(left_in)
        ]
        for copy in copies:
            copy.start()
        for copy in copies:
            copy.wait()

    rows = out.shape[0]
    at = pl.multiple_of(pl.program_id(0) * rows, rows)
    depth = left.shape[0] * left.shape[1] * left.shape[2]
    out[...] = lax.dot_general(
        left[:, :, :, pl.ds(at, rows)].reshape(depth, rows),
        right[...].reshape(depth, right.shape[3]),
        (((0,), (0,)), ((), ())),
        preferred_element_type=F32,
    )


def product(left, left_slots, right, right_slots):
    n_left, n_right = len(left), len(right)
    rows, cols = left[0].shape[2], right[0].shape[2]
    block = 256
    smem = pl.BlockSpec(memory_space=pltpu.SMEM)
    return pl.pallas_call(
        lambda *refs: product_kernel(n_left, n_right, *refs),
        grid=(rows // block,),
        in_specs=[smem, smem] + [pl.BlockSpec(memory_space=pl.ANY)] * (n_left + n_right),
        out_specs=pl.BlockSpec((block, cols), lambda m: (m, 0)),
        out_shape=jax.ShapeDtypeStruct((rows, cols), F32),
        scratch_shapes=[
            pltpu.VMEM((n_left,) + left[0].shape, BF),
            pltpu.VMEM((right[0].shape[0], n_right) + right[0].shape[1:], BF),
            pltpu.SemaphoreType.DMA((n_left,)),
            pltpu.SemaphoreType.DMA((n_right,)),
        ],
        compiler_params=pltpu.CompilerParams(vmem_limit_bytes=40 * 1024 * 1024),
        name="product",
    )(left_slots, right_slots, *left, *right)


RING = 4


def shift(value, axis, step, stride):
    count = lax.axis_size(axis)
    block = RING * stride

    def target(i):
        place = i // stride % RING
        return i // block * block + (place + step) % RING * stride + i % stride

    return lax.ppermute(value, axis, [(i, target(i)) for i in range(count)])


def swap(value, axis, bit):
    count = lax.axis_size(axis)
    return lax.ppermute(value, axis, [(i, i ^ bit) for i in range(count)])


def ring(value, axis, stride, forward):
    before = shift(value, axis, 1, stride)
    after = shift(value, axis, -1, stride)
    far = shift(before, axis, 1, stride) if forward else shift(after, axis, -1, stride)
    return [value, before, after, far]


def ring_places(index, stride):
    block = RING * stride
    place = index // stride % RING
    base = index - place * stride
    return [base + (place + step) % RING * stride for step in (0, RING - 1, 1, 2)]


def per_device(valence, conduction, valence_energy, conduction_energy, pair_list, sphere_index):
    n_row, n_col = lax.axis_size("row"), lax.axis_size("col")
    r, c = lax.axis_index("row"), lax.axis_index("col")
    left, right = densities(
        n_row, n_col, valence, conduction, valence_energy, conduction_energy, pair_list, sphere_index
    )
    right = lax.all_to_all(right, "col", split_axis=0, concat_axis=0, tiled=True)
    right_far = swap(right, "row", 4)
    rights = ring(right, "row", 1, True)
    left = lax.all_to_all(left, "row", split_axis=0, concat_axis=0, tiled=True)
    left_far = swap(left, "col", 2)
    lefts = ring(left, "col", 4, True)
    rights += ring(right_far, "row", 1, False)
    lefts += ring(left_far, "col", 4, False)
    lefts += [swap(piece, "col", 1) for piece in lefts]
    right_slots = ring_places(r, 1) + ring_places(r ^ 4, 1)
    left_slots = ring_places(c, 4) + ring_places(c ^ 2, 4)
    left_slots += [slot ^ 1 for slot in left_slots]
    return product(lefts, jnp.stack(left_slots), rights, jnp.stack(right_slots))


def solution(mesh):
    return jax.shard_map(
        per_device,
        mesh=mesh,
        in_specs=(
            P("row", None, None),
            P("col", None, None),
            P("row"),
            P("col"),
            P(("col", "row"), None),
            P(),
        ),
        out_specs=P("row", "col"),
        check_vma=False,
    )
```

```python
import math

import jax
import jax.numpy as jnp
import numpy as np
from jax import lax
from jax.experimental import pallas as pl
from jax.experimental.pallas import tpu as pltpu
from jax.sharding import PartitionSpec as P

EDGE = 64
HALF = EDGE // 2
LANES = 128
BF = jnp.bfloat16
F32 = jnp.float32


def two_terms(table):
    high = table.astype(np.float32).astype(BF)
    low = (table - high.astype(np.float64)).astype(BF)
    return np.asarray(high), np.asarray(low)


def x_table():
    x = np.arange(EDGE)
    a = np.arange(HALF)
    angle = 2.0 * np.pi * ((a[:, None] * x[None, :]) % EDGE) / EDGE
    table = np.concatenate([np.cos(angle), -np.sin(angle)], axis=0)
    table[HALF] = 1.0 - 2.0 * (x % 2)
    high, low = two_terms(table)
    return np.concatenate([high, high, low], axis=1)


def z_table():
    z = np.arange(EDGE)
    angle = 2.0 * np.pi * ((z[:, None] * z[None, :]) % EDGE) / EDGE
    table = np.concatenate([np.cos(angle), np.sin(angle)], axis=1) * EDGE ** (-1.5)
    high, low = two_terms(table)
    return np.block([[high, high], [low, np.zeros_like(low)]]).astype(BF)


def y_table():
    angle = 2.0 * np.pi * np.arange(HALF) / EDGE
    odd = np.arange(LANES)[None, :] >= EDGE
    real = np.where(odd, np.cos(angle)[:, None], 1.0)
    imag = np.where(odd, -np.sin(angle)[:, None], 0.0)
    return np.concatenate([real, imag], axis=0).astype(np.float32)


def small_dft(re, im):
    n = len(re)
    if n == 1:
        return re, im
    even_re, even_im = small_dft(re[0::2], im[0::2])
    odd_re, odd_im = small_dft(re[1::2], im[1::2])
    out_re, out_im = [None] * n, [None] * n
    for k in range(n // 2):
        r, i = odd_re[k], odd_im[k]
        if k == 0:
            pass
        elif 4 * k == n:
            r, i = i, -r
        elif 8 * k == n:
            s = math.sqrt(0.5)
            r, i = (r + i) * s, (i - r) * s
        elif 8 * k == 3 * n:
            s = math.sqrt(0.5)
            r, i = (i - r) * s, (r + i) * -s
        else:
            c, s = math.cos(2 * math.pi * k / n), math.sin(2 * math.pi * k / n)
            r, i = r * c + i * s, i * c - r * s
        out_re[k], out_im[k] = even_re[k] + r, even_im[k] + i
        out_re[k + n // 2], out_im[k + n // 2] = even_re[k] - r, even_im[k] - i
    return out_re, out_im


def split(value):
    high = value.astype(BF)
    return high, (value - high.astype(F32)).astype(BF)


def half_space(index):
    a, b, c = index >> 12, (index >> 6) & (EDGE - 1), index & (EDGE - 1)
    mirrored = a > HALF
    a = jnp.where(mirrored, EDGE - a, a)
    b = jnp.where(mirrored, (EDGE - b) & (EDGE - 1), b)
    c = jnp.where(mirrored, (EDGE - c) & (EDGE - 1), c)
    return a, b, c, mirrored


def density_kernel(
    total_pairs,
    valence_hbm,
    conduction_hbm,
    valence_energy_hbm,
    conduction_energy_hbm,
    pairs_hbm,
    wave_hbm,
    x_factors_hbm,
    z_factors_hbm,
    y_factors_hbm,
    left,
    right,
    staged,
    table,
    valence,
    conduction,
    valence_energy,
    conduction_energy,
    pairs,
    wave,
    rows_vector,
    rows,
    x_factors,
    z_factors,
    y_factors,
    picked_0,
    picked_1,
    sems,
    orbital_sems,
):
    n_pairs = 8
    wide = 2 * LANES
    groups = orbital_sems.shape[1]
    span = EDGE * EDGE // groups

    small = [
        pltpu.make_async_copy(src, dst, sems.at[i])
        for i, (src, dst) in enumerate(
            [
                (pairs_hbm, pairs),
                (x_factors_hbm, x_factors),
                (wave_hbm, wave),
                (valence_energy_hbm, valence_energy),
                (conduction_energy_hbm, conduction_energy),
                (z_factors_hbm, z_factors),
                (y_factors_hbm, y_factors),
            ]
        )
    ]
    for copy in small:
        copy.start()
    orbitals = []
    for n in range(groups):
        at = pl.ds(n * span, span)
        orbitals.append(
            [
                pltpu.make_async_copy(valence_hbm.at[:, :, at], valence.at[:, :, at], orbital_sems.at[0, n]),
                pltpu.make_async_copy(conduction_hbm.at[:, :, at], conduction.at[:, :, at], orbital_sems.at[1, n]),
            ]
        )
        for copy in orbitals[-1]:
            copy.start()
    for copy in small:
        copy.wait()

    a, b, c, _ = half_space(wave[...])
    rows_vector[...] = (a * 8 + (b >> 3)) * EDGE + c
    to_scalar = pltpu.make_async_copy(rows_vector, rows, sems.at[0])
    to_scalar.start()

    v_local = [lax.rem(pairs[0, p], valence.shape[0]) for p in range(n_pairs)]
    c_local = [lax.rem(pairs[1, p], conduction.shape[0]) for p in range(n_pairs)]
    sublane = lax.broadcasted_iota(jnp.int32, (8, LANES), 0)
    gap = jnp.ones((8, LANES), F32)
    for p in range(n_pairs):
        gap = jnp.where(sublane == p, conduction_energy[c_local[p]] - valence_energy[v_local[p]], gap)
    w = -4.0 / (total_pairs * gap)

    def x_stage(chunk, carry):
        lanes = pl.ds(pl.multiple_of(chunk * wide, wide), wide)
        for p in range(n_pairs):
            product = valence[v_local[p], :, lanes] * conduction[c_local[p], :, lanes]
            high, low = split(product)
            spectrum = jnp.dot(
                x_factors[...],
                jnp.concatenate([high, low, high], axis=0),
                preferred_element_type=F32,
            )
            for h in range(2):
                staged[2 * chunk + h, pl.ds(p, EDGE, stride=8), :] = spectrum[:, h * LANES : (h + 1) * LANES]
        return carry

    for n in range(groups):
        for copy in orbitals[n]:
            copy.wait()
        lax.fori_loop(n * span // wide, (n + 1) * span // wide, x_stage, 0)

    first = lax.broadcasted_iota(jnp.int32, (8, LANES), 1) < EDGE

    def yz_stage(a, carry):
        complex_plane = jnp.where((a & (HALF - 1)) == 0, 0.0, 1.0)
        at_re = pl.ds(pl.multiple_of(a * 8, 8), 8)
        at_im = pl.ds(pl.multiple_of(((a & (HALF - 1)) + HALF) * 8, 8), 8)
        re = [staged[y, at_re, :] for y in range(HALF)]
        im = [staged[y, at_im, :] * complex_plane for y in range(HALF)]
        re, im = small_dft(re, im)
        lower, upper = [], []
        for b in range(HALF):
            r, i = re[b], im[b]
            if b:
                c = y_factors[pl.ds(b, 8, stride=0), :]
                s = y_factors[pl.ds(b + HALF, 8, stride=0), :]
                r, i = r * c - i * s, r * s + i * c
            even = jnp.where(first, r, pltpu.roll(i, EDGE, 1))
            odd = jnp.where(first, pltpu.roll(r, EDGE, 1), i)
            for part, line in ((lower, even + odd), (upper, even - odd)):
                turned = pltpu.roll(line, EDGE, 1)
                part += [line, jnp.where(first, turned, -turned)]
        high, low = split(jnp.concatenate(lower + upper, axis=0))
        out = lax.dot_general(
            z_factors[...],
            jnp.concatenate([high, low], axis=1),
            (((1,), (1,)), ((), ())),
            preferred_element_type=F32,
        )
        out = out[:EDGE] + out[EDGE:]
        for n in range(8):
            at = pl.multiple_of((a * 8 + n) * EDGE, EDGE)
            table[pl.ds(at, EDGE), :] = out[:, n * LANES : (n + 1) * LANES]
        return carry

    lax.fori_loop(0, HALF + 1, yz_stage, 0)

    to_scalar.wait()
    per_row, per_col = left.shape[2] // LANES, right.shape[2] // LANES

    def pick(q, picked):
        for j in range(LANES):
            picked[pl.ds(j, 1), :] = table[pl.ds(rows[q, j], 1), :]

    def finish(q, picked):
        turned = picked[...].T
        _, b, _, mirrored = half_space(wave[pl.ds(q, 8, stride=0), :])
        bits = [(b & (1 << i)) != 0 for i in range(3)]
        parts = []
        for k in range(2):
            some = [turned[n * 16 + k * 8 : n * 16 + k * 8 + 8] for n in range(8)]
            for bit in bits:
                some = [jnp.where(bit, some[n + 1], some[n]) for n in range(0, len(some), 2)]
            parts.append(some[0])
        re, im = parts
        im = jnp.where(mirrored, -im, im)
        plain = jnp.concatenate([re, im], axis=0).astype(BF)
        scaled = jnp.concatenate([w * re, w * im], axis=0).astype(BF)
        at = pl.multiple_of((q % per_row) * LANES, LANES)
        left[q // per_row, :, pl.ds(at, LANES)] = scaled
        at = pl.multiple_of((q % per_col) * LANES, LANES)
        right[q // per_col, :, pl.ds(at, LANES)] = plain

    count = wave.shape[0]
    pick(0, picked_0)

    def select(i, carry):
        pick(2 * i + 1, picked_1)
        finish(2 * i, picked_0)
        pick(jnp.minimum(2 * i + 2, count - 1), picked_0)
        finish(2 * i + 1, picked_1)
        return carry

    lax.fori_loop(0, count // 2, select, 0)


def densities(n_row, n_col, valence, conduction, valence_energy, conduction_energy, pair_list, sphere_index):
    n_pairs, waves = pair_list.shape[0], sphere_index.shape[0]
    tables = [jnp.asarray(x_table()), jnp.asarray(z_table()), jnp.asarray(y_table())]
    hbm = pl.BlockSpec(memory_space=pltpu.HBM)
    vmem = pl.BlockSpec(memory_space=pltpu.VMEM)
    return pl.pallas_call(
        lambda *refs: density_kernel(n_pairs * n_row * n_col, *refs),
        in_specs=[hbm] * 9,
        out_specs=[vmem, vmem],
        out_shape=[
            jax.ShapeDtypeStruct((n_row, 2 * n_pairs, waves // n_row), BF),
            jax.ShapeDtypeStruct((n_col, 2 * n_pairs, waves // n_col), BF),
        ],
        scratch_shapes=[
            pltpu.VMEM((HALF, n_pairs * EDGE, LANES), F32),
            pltpu.VMEM(((HALF + 1) * 8 * EDGE, LANES), F32),
            pltpu.VMEM(valence.shape, F32),
            pltpu.VMEM(conduction.shape, F32),
            pltpu.SMEM(valence_energy.shape, F32),
            pltpu.SMEM(conduction_energy.shape, F32),
            pltpu.SMEM((2, n_pairs), jnp.int32),
            pltpu.VMEM((waves // LANES, LANES), jnp.int32),
            pltpu.VMEM((waves // LANES, LANES), jnp.int32),
            pltpu.SMEM((waves // LANES, LANES), jnp.int32),
            pltpu.VMEM(tables[0].shape, BF),
            pltpu.VMEM(tables[1].shape, BF),
            pltpu.VMEM(tables[2].shape, F32),
            pltpu.VMEM((LANES, LANES), F32),
            pltpu.VMEM((LANES, LANES), F32),
            pltpu.SemaphoreType.DMA((7,)),
            pltpu.SemaphoreType.DMA((2, 4)),
        ],
        compiler_params=pltpu.CompilerParams(vmem_limit_bytes=60 * 1024 * 1024),
        name="density",
    )(
        valence,
        conduction,
        valence_energy,
        conduction_energy,
        pair_list.T,
        sphere_index.reshape(-1, LANES),
        *tables,
    )


def product_kernel(n_left, n_right, *refs):
    left_in, right_in = refs[:n_left], refs[n_left : n_left + n_right]
    out, left, right, left_sem, right_sem = refs[n_left + n_right :]

    @pl.when(pl.program_id(0) == 0)
    def _():
        left_slots, right_slots = left_places(lax.axis_index("col")), right_places(lax.axis_index("row"))
        copies = [
            pltpu.make_async_copy(piece, right.at[:, right_slots[j]], right_sem.at[j])
            for j, piece in enumerate(right_in)
        ] + [
            pltpu.make_async_copy(piece, left.at[left_slots[i]], left_sem.at[i])
            for i, piece in enumerate(left_in)
        ]
        for copy in copies:
            copy.start()
        for copy in copies:
            copy.wait()

    rows = out.shape[0]
    at = pl.multiple_of(pl.program_id(0) * rows, rows)
    depth = left.shape[0] * left.shape[1] * left.shape[2]
    out[...] = lax.dot_general(
        left[:, :, :, pl.ds(at, rows)].reshape(depth, rows),
        right[...].reshape(depth, right.shape[3]),
        (((0,), (0,)), ((), ())),
        preferred_element_type=F32,
    )


def product(left, right):
    n_left, n_right = len(left), len(right)
    rows, cols = left[0].shape[2], right[0].shape[2]
    block = 256
    return pl.pallas_call(
        lambda *refs: product_kernel(n_left, n_right, *refs),
        grid=(rows // block,),
        in_specs=[pl.BlockSpec(memory_space=pl.ANY)] * (n_left + n_right),
        out_specs=pl.BlockSpec((block, cols), lambda m: (m, 0)),
        out_shape=jax.ShapeDtypeStruct((rows, cols), F32),
        scratch_shapes=[
            pltpu.VMEM((n_left,) + left[0].shape, BF),
            pltpu.VMEM((right[0].shape[0], n_right) + right[0].shape[1:], BF),
            pltpu.SemaphoreType.DMA((n_left,)),
            pltpu.SemaphoreType.DMA((n_right,)),
        ],
        compiler_params=pltpu.CompilerParams(vmem_limit_bytes=24 * 1024 * 1024),
        name="product",
    )(*left, *right)


RING = 4


def shift(value, axis, step, stride):
    count = lax.axis_size(axis)
    block = RING * stride

    def target(i):
        place = i // stride % RING
        return i // block * block + (place + step) % RING * stride + i % stride

    return lax.ppermute(value, axis, [(i, target(i)) for i in range(count)])


def swap(value, axis, bit):
    count = lax.axis_size(axis)
    return lax.ppermute(value, axis, [(i, i ^ bit) for i in range(count)])


def ring(value, axis, stride, forward):
    before = shift(value, axis, 1, stride)
    after = shift(value, axis, -1, stride)
    far = shift(before, axis, 1, stride) if forward else shift(after, axis, -1, stride)
    return [value, before, after, far]


def ring_places(index, stride):
    place = lax.rem(lax.div(index, stride), RING)
    base = index - place * stride
    return [base + lax.rem(place + step, RING) * stride for step in (0, RING - 1, 1, 2)]


def right_places(row):
    return ring_places(row, 1) + ring_places(row ^ RING, 1)


def left_places(col):
    places = ring_places(col, RING) + ring_places(col ^ 2, RING)
    return places + [place ^ 1 for place in places]


def per_device(valence, conduction, valence_energy, conduction_energy, pair_list, sphere_index):
    n_row, n_col = lax.axis_size("row"), lax.axis_size("col")
    left, right = densities(
        n_row, n_col, valence, conduction, valence_energy, conduction_energy, pair_list, sphere_index
    )
    right = lax.all_to_all(right, "col", split_axis=0, concat_axis=0, tiled=True)
    right_far = swap(right, "row", 4)
    rights = ring(right, "row", 1, True)
    left = lax.all_to_all(left, "row", split_axis=0, concat_axis=0, tiled=True)
    left_far = swap(left, "col", 2)
    lefts = ring(left, "col", 4, True)
    rights += ring(right_far, "row", 1, False)
    lefts += ring(left_far, "col", 4, False)
    lefts += [swap(piece, "col", 1) for piece in lefts]
    return product(lefts, rights)


def solution(mesh):
    return jax.shard_map(
        per_device,
        mesh=mesh,
        in_specs=(
            P("row", None, None),
            P("col", None, None),
            P("row"),
            P("col"),
            P(("col", "row"), None),
            P(),
        ),
        out_specs=P("row", "col"),
        check_vma=False,
    )
```

```python
import math

import jax
import jax.numpy as jnp
import numpy as np
from jax import lax
from jax.experimental import pallas as pl
from jax.experimental.pallas import tpu as pltpu
from jax.sharding import PartitionSpec as P

EDGE = 64
HALF = EDGE // 2
LANES = 128
BF = jnp.bfloat16
F32 = jnp.float32


def two_terms(table):
    high = table.astype(np.float32).astype(BF)
    low = (table - high.astype(np.float64)).astype(BF)
    return np.asarray(high), np.asarray(low)


def x_table():
    x = np.arange(EDGE)
    a = np.arange(HALF)
    angle = 2.0 * np.pi * ((a[:, None] * x[None, :]) % EDGE) / EDGE
    table = np.concatenate([np.cos(angle), -np.sin(angle)], axis=0)
    table[HALF] = 1.0 - 2.0 * (x % 2)
    high, low = two_terms(table)
    return np.concatenate([high, high, low], axis=1)


def z_table():
    z = np.arange(EDGE)
    angle = 2.0 * np.pi * ((z[:, None] * z[None, :]) % EDGE) / EDGE
    table = np.concatenate([np.cos(angle), np.sin(angle)], axis=1) * EDGE ** (-1.5)
    high, low = two_terms(table)
    return np.block([[high, high], [low, np.zeros_like(low)]]).astype(BF)


def y_table():
    angle = 2.0 * np.pi * np.arange(HALF) / EDGE
    odd = np.arange(LANES)[None, :] >= EDGE
    real = np.where(odd, np.cos(angle)[:, None], 1.0)
    imag = np.where(odd, -np.sin(angle)[:, None], 0.0)
    return np.concatenate([real, imag], axis=0).astype(np.float32)


def small_dft(re, im):
    n = len(re)
    if n == 1:
        return re, im
    even_re, even_im = small_dft(re[0::2], im[0::2])
    odd_re, odd_im = small_dft(re[1::2], im[1::2])
    out_re, out_im = [None] * n, [None] * n
    for k in range(n // 2):
        r, i = odd_re[k], odd_im[k]
        if k == 0:
            pass
        elif 4 * k == n:
            r, i = i, -r
        elif 8 * k == n:
            s = math.sqrt(0.5)
            r, i = (r + i) * s, (i - r) * s
        elif 8 * k == 3 * n:
            s = math.sqrt(0.5)
            r, i = (i - r) * s, (r + i) * -s
        else:
            c, s = math.cos(2 * math.pi * k / n), math.sin(2 * math.pi * k / n)
            r, i = r * c + i * s, i * c - r * s
        out_re[k], out_im[k] = even_re[k] + r, even_im[k] + i
        out_re[k + n // 2], out_im[k + n // 2] = even_re[k] - r, even_im[k] - i
    return out_re, out_im


def split(value):
    high = value.astype(BF)
    return high, (value - high.astype(F32)).astype(BF)


def half_space(index):
    a, b, c = index >> 12, (index >> 6) & (EDGE - 1), index & (EDGE - 1)
    mirrored = a > HALF
    a = jnp.where(mirrored, EDGE - a, a)
    b = jnp.where(mirrored, (EDGE - b) & (EDGE - 1), b)
    c = jnp.where(mirrored, (EDGE - c) & (EDGE - 1), c)
    return a, b, c, mirrored


def density_kernel(
    total_pairs,
    valence_hbm,
    conduction_hbm,
    valence_energy_hbm,
    conduction_energy_hbm,
    pairs_hbm,
    wave_hbm,
    x_factors_hbm,
    z_factors_hbm,
    y_factors_hbm,
    left,
    right,
    staged,
    table,
    valence,
    conduction,
    valence_energy,
    conduction_energy,
    pairs,
    wave,
    rows_vector,
    rows,
    x_factors,
    z_factors,
    y_factors,
    picked_0,
    picked_1,
    sems,
    orbital_sems,
):
    n_pairs = 8
    wide = 2 * LANES
    groups = orbital_sems.shape[1]
    span = EDGE * EDGE // groups

    small = [
        pltpu.make_async_copy(src, dst, sems.at[i])
        for i, (src, dst) in enumerate(
            [
                (pairs_hbm, pairs),
                (x_factors_hbm, x_factors),
                (wave_hbm, wave),
                (valence_energy_hbm, valence_energy),
                (conduction_energy_hbm, conduction_energy),
                (z_factors_hbm, z_factors),
                (y_factors_hbm, y_factors),
            ]
        )
    ]
    for copy in small:
        copy.start()
    orbitals = []
    for n in range(groups):
        at = pl.ds(n * span, span)
        orbitals.append(
            [
                pltpu.make_async_copy(valence_hbm.at[:, :, at], valence.at[:, :, at], orbital_sems.at[0, n]),
                pltpu.make_async_copy(conduction_hbm.at[:, :, at], conduction.at[:, :, at], orbital_sems.at[1, n]),
            ]
        )
        for copy in orbitals[-1]:
            copy.start()
    for copy in small:
        copy.wait()

    a, b, c, _ = half_space(wave[...])
    rows_vector[...] = (a * 8 + (b >> 3)) * EDGE + c
    to_scalar = pltpu.make_async_copy(rows_vector, rows, sems.at[0])
    to_scalar.start()

    v_local = [lax.rem(pairs[0, p], valence.shape[0]) for p in range(n_pairs)]
    c_local = [lax.rem(pairs[1, p], conduction.shape[0]) for p in range(n_pairs)]
    sublane = lax.broadcasted_iota(jnp.int32, (8, LANES), 0)
    gap = jnp.ones((8, LANES), F32)
    for p in range(n_pairs):
        gap = jnp.where(sublane == p, conduction_energy[c_local[p]] - valence_energy[v_local[p]], gap)
    w = -4.0 / (total_pairs * gap)

    def x_stage(chunk, carry):
        lanes = pl.ds(pl.multiple_of(chunk * wide, wide), wide)
        for p in range(n_pairs):
            product = valence[v_local[p], :, lanes] * conduction[c_local[p], :, lanes]
            high, low = split(product)
            spectrum = jnp.dot(
                x_factors[...],
                jnp.concatenate([high, low, high], axis=0),
                preferred_element_type=F32,
            )
            for h in range(2):
                staged[2 * chunk + h, pl.ds(p, EDGE, stride=8), :] = spectrum[:, h * LANES : (h + 1) * LANES]
        return carry

    for n in range(groups):
        for copy in orbitals[n]:
            copy.wait()
        lax.fori_loop(n * span // wide, (n + 1) * span // wide, x_stage, 0)

    first = lax.broadcasted_iota(jnp.int32, (8, LANES), 1) < EDGE

    def yz_stage(a, carry):
        complex_plane = jnp.where((a & (HALF - 1)) == 0, 0.0, 1.0)
        at_re = pl.ds(pl.multiple_of(a * 8, 8), 8)
        at_im = pl.ds(pl.multiple_of(((a & (HALF - 1)) + HALF) * 8, 8), 8)
        re = [staged[y, at_re, :] for y in range(HALF)]
        im = [staged[y, at_im, :] * complex_plane for y in range(HALF)]
        re, im = small_dft(re, im)
        lower, upper = [], []
        for b in range(HALF):
            r, i = re[b], im[b]
            if b:
                c = y_factors[pl.ds(b, 8, stride=0), :]
                s = y_factors[pl.ds(b + HALF, 8, stride=0), :]
                r, i = r * c - i * s, r * s + i * c
            even = jnp.where(first, r, pltpu.roll(i, EDGE, 1))
            odd = jnp.where(first, pltpu.roll(r, EDGE, 1), i)
            for part, line in ((lower, even + odd), (upper, even - odd)):
                turned = pltpu.roll(line, EDGE, 1)
                part += [line, jnp.where(first, turned, -turned)]
        high, low = split(jnp.concatenate(lower + upper, axis=0))
        out = lax.dot_general(
            z_factors[...],
            jnp.concatenate([high, low], axis=1),
            (((1,), (1,)), ((), ())),
            preferred_element_type=F32,
        )
        out = out[:EDGE] + out[EDGE:]
        for n in range(8):
            at = pl.multiple_of((a * 8 + n) * EDGE, EDGE)
            table[pl.ds(at, EDGE), :] = out[:, n * LANES : (n + 1) * LANES]
        return carry

    lax.fori_loop(0, HALF + 1, yz_stage, 0)

    to_scalar.wait()
    per_row, per_col = left.shape[2] // LANES, right.shape[2] // LANES

    def pick(q, picked):
        for j in range(LANES):
            picked[pl.ds(j, 1), :] = table[pl.ds(rows[q, j], 1), :]

    def finish(q, picked):
        turned = picked[...].T
        _, b, _, mirrored = half_space(wave[pl.ds(q, 8, stride=0), :])
        bits = [(b & (1 << i)) != 0 for i in range(3)]
        parts = []
        for k in range(2):
            some = [turned[n * 16 + k * 8 : n * 16 + k * 8 + 8] for n in range(8)]
            for bit in bits:
                some = [jnp.where(bit, some[n + 1], some[n]) for n in range(0, len(some), 2)]
            parts.append(some[0])
        re, im = parts
        im = jnp.where(mirrored, -im, im)
        plain = jnp.concatenate([re, im], axis=0).astype(BF)
        scaled = jnp.concatenate([w * re, w * im], axis=0).astype(BF)
        at = pl.multiple_of((q % per_row) * LANES, LANES)
        left[q // per_row, :, pl.ds(at, LANES)] = scaled
        at = pl.multiple_of((q % per_col) * LANES, LANES)
        right[q // per_col, :, pl.ds(at, LANES)] = plain

    count = wave.shape[0]
    pick(0, picked_0)

    def select(i, carry):
        pick(2 * i + 1, picked_1)
        finish(2 * i, picked_0)
        pick(jnp.minimum(2 * i + 2, count - 1), picked_0)
        finish(2 * i + 1, picked_1)
        return carry

    lax.fori_loop(0, count // 2, select, 0)


def densities(n_row, n_col, valence, conduction, valence_energy, conduction_energy, pair_list, sphere_index):
    n_pairs, waves = pair_list.shape[0], sphere_index.shape[0]
    tables = [jnp.asarray(x_table()), jnp.asarray(z_table()), jnp.asarray(y_table())]
    hbm = pl.BlockSpec(memory_space=pltpu.HBM)
    vmem = pl.BlockSpec(memory_space=pltpu.VMEM)
    return pl.pallas_call(
        lambda *refs: density_kernel(n_pairs * n_row * n_col, *refs),
        in_specs=[hbm] * 9,
        out_specs=[vmem, vmem],
        out_shape=[
            jax.ShapeDtypeStruct((n_row, 2 * n_pairs, waves // n_row), BF),
            jax.ShapeDtypeStruct((n_col, 2 * n_pairs, waves // n_col), BF),
        ],
        scratch_shapes=[
            pltpu.VMEM((HALF, n_pairs * EDGE, LANES), F32),
            pltpu.VMEM(((HALF + 1) * 8 * EDGE, LANES), F32),
            pltpu.VMEM(valence.shape, F32),
            pltpu.VMEM(conduction.shape, F32),
            pltpu.SMEM(valence_energy.shape, F32),
            pltpu.SMEM(conduction_energy.shape, F32),
            pltpu.SMEM((2, n_pairs), jnp.int32),
            pltpu.VMEM((waves // LANES, LANES), jnp.int32),
            pltpu.VMEM((waves // LANES, LANES), jnp.int32),
            pltpu.SMEM((waves // LANES, LANES), jnp.int32),
            pltpu.VMEM(tables[0].shape, BF),
            pltpu.VMEM(tables[1].shape, BF),
            pltpu.VMEM(tables[2].shape, F32),
            pltpu.VMEM((LANES, LANES), F32),
            pltpu.VMEM((LANES, LANES), F32),
            pltpu.SemaphoreType.DMA((7,)),
            pltpu.SemaphoreType.DMA((2, 4)),
        ],
        compiler_params=pltpu.CompilerParams(vmem_limit_bytes=60 * 1024 * 1024),
        name="density",
    )(
        valence,
        conduction,
        valence_energy,
        conduction_energy,
        pair_list.T,
        sphere_index.reshape(-1, LANES),
        *tables,
    )


def product_kernel(n_left, n_right, *refs):
    left_in, right_in = refs[:n_left], refs[n_left : n_left + n_right]
    out, left, right, left_sem, right_sem = refs[n_left + n_right :]

    @pl.when(pl.program_id(0) == 0)
    def _():
        col = lax.axis_index("col")
        left_slots, right_slots = left_places(col), right_places(lax.axis_index("row"), col & 1)
        copies = [
            pltpu.make_async_copy(piece, right.at[:, right_slots[j]], right_sem.at[j])
            for j, piece in enumerate(right_in)
        ] + [
            pltpu.make_async_copy(piece, left.at[left_slots[i]], left_sem.at[i])
            for i, piece in enumerate(left_in)
        ]
        for copy in copies:
            copy.start()
        for copy in copies:
            copy.wait()

    rows = out.shape[0]
    at = pl.multiple_of(pl.program_id(0) * rows, rows)
    depth = left.shape[0] * left.shape[1] * left.shape[2]
    out[...] = lax.dot_general(
        left[:, :, :, pl.ds(at, rows)].reshape(depth, rows),
        right[...].reshape(depth, right.shape[3]),
        (((0,), (0,)), ((), ())),
        preferred_element_type=F32,
    )


def product(left, right):
    n_left, n_right = len(left), len(right)
    rows, cols = left[0].shape[2], right[0].shape[2]
    block = 256
    return pl.pallas_call(
        lambda *refs: product_kernel(n_left, n_right, *refs),
        grid=(rows // block,),
        in_specs=[pl.BlockSpec(memory_space=pl.ANY)] * (n_left + n_right),
        out_specs=pl.BlockSpec((block, cols), lambda m: (m, 0)),
        out_shape=jax.ShapeDtypeStruct((rows, cols), F32),
        scratch_shapes=[
            pltpu.VMEM((n_left,) + left[0].shape, BF),
            pltpu.VMEM((right[0].shape[0], n_right) + right[0].shape[1:], BF),
            pltpu.SemaphoreType.DMA((n_left,)),
            pltpu.SemaphoreType.DMA((n_right,)),
        ],
        compiler_params=pltpu.CompilerParams(vmem_limit_bytes=24 * 1024 * 1024),
        name="product",
    )(*left, *right)


RING = 4


def shift(value, axis, stride, way):
    n_col, n_row = lax.axis_size("col"), lax.axis_size("row")

    def moved(i, step):
        place = i // stride % RING
        return i + ((place + step) % RING - place) * stride

    pairs = []
    for col in range(n_col):
        for row in range(n_row):
            step = way if col % 2 == 0 else -way
            to = (moved(col, step), row) if axis == "col" else (col, moved(row, step))
            pairs.append((col * n_row + row, to[0] * n_row + to[1]))
    return lax.ppermute(value, ("col", "row"), pairs)


def swap(value, axis, bit):
    count = lax.axis_size(axis)
    return lax.ppermute(value, axis, [(i, i ^ bit) for i in range(count)])


def ring_places(index, stride, core):
    place = lax.rem(lax.div(index, stride), RING)
    base = index - place * stride
    way = 1 - 2 * core
    return [base + lax.rem(place + step, RING) * stride for step in (0, RING - way, RING + way, 2)]


def right_places(row, core):
    return ring_places(row, 1, core) + ring_places(row ^ RING, 1, core)


def left_places(col):
    core = col & 1
    mine = ring_places(col, RING, core) + ring_places(col ^ 2, RING, core)
    theirs = ring_places(col ^ 1, RING, 1 - core) + ring_places(col ^ 3, RING, 1 - core)
    return mine + theirs


def per_device(valence, conduction, valence_energy, conduction_energy, pair_list, sphere_index):
    n_row, n_col = lax.axis_size("row"), lax.axis_size("col")
    left, right = densities(
        n_row, n_col, valence, conduction, valence_energy, conduction_energy, pair_list, sphere_index
    )
    left = lax.all_to_all(left, "row", split_axis=0, concat_axis=0, tiled=True)
    left, right = lax.optimization_barrier((left, right))
    left_z = swap(left, "col", 2)
    lefts = [left, shift(left, "col", RING, 1), shift(left, "col", RING, -1)]
    right = lax.all_to_all(right, "col", split_axis=0, concat_axis=0, tiled=True)
    right_z = swap(right, "row", RING)
    rights = [right, shift(right, "row", 1, 1), shift(right, "row", 1, -1)]
    lefts += [shift(lefts[1], "col", RING, 1), left_z, shift(left_z, "col", RING, 1), shift(left_z, "col", RING, -1)]
    rights += [shift(rights[1], "row", 1, 1), right_z, shift(right_z, "row", 1, 1), shift(right_z, "row", 1, -1)]
    lefts += [shift(lefts[5], "col", RING, 1)]
    rights += [shift(rights[5], "row", 1, 1)]
    lefts += [swap(piece, "col", 1) for piece in lefts]
    return product(lefts, rights)


def solution(mesh):
    return jax.shard_map(
        per_device,
        mesh=mesh,
        in_specs=(
            P("row", None, None),
            P("col", None, None),
            P("row"),
            P("col"),
            P(("col", "row"), None),
            P(),
        ),
        out_specs=P("row", "col"),
        check_vma=False,
    )
```

```python
import math

import jax
import jax.numpy as jnp
import numpy as np
from jax import lax
from jax.experimental import pallas as pl
from jax.experimental.pallas import tpu as pltpu
from jax.sharding import PartitionSpec as P

EDGE = 64
HALF = EDGE // 2
LANES = 128
BF = jnp.bfloat16
F32 = jnp.float32


def two_terms(table):
    high = table.astype(np.float32).astype(BF)
    low = (table - high.astype(np.float64)).astype(BF)
    return np.asarray(high), np.asarray(low)


def x_table():
    x = np.arange(EDGE)
    a = np.arange(HALF)
    angle = 2.0 * np.pi * ((a[:, None] * x[None, :]) % EDGE) / EDGE
    table = np.concatenate([np.cos(angle), -np.sin(angle)], axis=0)
    table[HALF] = 1.0 - 2.0 * (x % 2)
    high, low = two_terms(table)
    return np.concatenate([high, high, low], axis=1)


def z_table():
    z = np.arange(EDGE)
    angle = 2.0 * np.pi * ((z[:, None] * z[None, :]) % EDGE) / EDGE
    cosine, sine = np.cos(angle), np.sin(angle)
    table = np.block([[cosine, sine], [-sine, cosine]]) * EDGE ** (-1.5)
    high, low = two_terms(table)
    return np.block([[high, high], [low, np.zeros_like(low)]]).astype(BF)


def y_table():
    angle = 2.0 * np.pi * np.arange(HALF) / EDGE
    odd = np.arange(LANES)[None, :] >= EDGE
    real = np.where(odd, np.cos(angle)[:, None], 1.0)
    imag = np.where(odd, -np.sin(angle)[:, None], 0.0)
    return np.concatenate([real, imag], axis=0).astype(np.float32)


def small_dft(re, im):
    n = len(re)
    if n == 1:
        return re, im
    even_re, even_im = small_dft(re[0::2], im[0::2])
    odd_re, odd_im = small_dft(re[1::2], im[1::2])
    out_re, out_im = [None] * n, [None] * n
    for k in range(n // 2):
        r, i = odd_re[k], odd_im[k]
        if k == 0:
            pass
        elif 4 * k == n:
            r, i = i, -r
        elif 8 * k == n:
            s = math.sqrt(0.5)
            r, i = (r + i) * s, (i - r) * s
        elif 8 * k == 3 * n:
            s = math.sqrt(0.5)
            r, i = (i - r) * s, (r + i) * -s
        else:
            c, s = math.cos(2 * math.pi * k / n), math.sin(2 * math.pi * k / n)
            r, i = r * c + i * s, i * c - r * s
        out_re[k], out_im[k] = even_re[k] + r, even_im[k] + i
        out_re[k + n // 2], out_im[k + n // 2] = even_re[k] - r, even_im[k] - i
    return out_re, out_im


def split(value):
    high = value.astype(BF)
    return high, (value - high.astype(F32)).astype(BF)


def half_space(index):
    a, b, c = index >> 12, (index >> 6) & (EDGE - 1), index & (EDGE - 1)
    mirrored = a > HALF
    a = jnp.where(mirrored, EDGE - a, a)
    b = jnp.where(mirrored, (EDGE - b) & (EDGE - 1), b)
    c = jnp.where(mirrored, (EDGE - c) & (EDGE - 1), c)
    return a, b, c, mirrored


def density_kernel(
    total_pairs,
    valence_hbm,
    conduction_hbm,
    valence_energy_hbm,
    conduction_energy_hbm,
    pairs_hbm,
    wave_hbm,
    x_factors_hbm,
    z_factors_hbm,
    y_factors_hbm,
    left,
    right,
    staged,
    table,
    valence,
    conduction,
    valence_energy,
    conduction_energy,
    pairs,
    wave,
    rows_vector,
    rows,
    x_factors,
    z_factors,
    y_factors,
    picked_0,
    picked_1,
    sems,
    orbital_sems,
):
    n_pairs = 8
    wide = 2 * LANES
    groups = orbital_sems.shape[1]
    span = EDGE * EDGE // groups

    small = [
        pltpu.make_async_copy(src, dst, sems.at[i])
        for i, (src, dst) in enumerate(
            [
                (pairs_hbm, pairs),
                (x_factors_hbm, x_factors),
                (wave_hbm, wave),
                (valence_energy_hbm, valence_energy),
                (conduction_energy_hbm, conduction_energy),
                (z_factors_hbm, z_factors),
                (y_factors_hbm, y_factors),
            ]
        )
    ]
    for copy in small:
        copy.start()
    orbitals = []
    for n in range(groups):
        at = pl.ds(n * span, span)
        orbitals.append(
            [
                pltpu.make_async_copy(valence_hbm.at[:, :, at], valence.at[:, :, at], orbital_sems.at[0, n]),
                pltpu.make_async_copy(conduction_hbm.at[:, :, at], conduction.at[:, :, at], orbital_sems.at[1, n]),
            ]
        )
        for copy in orbitals[-1]:
            copy.start()
    for copy in small:
        copy.wait()

    a, b, c, _ = half_space(wave[...])
    rows_vector[...] = (a * 8 + (b >> 3)) * EDGE + c
    to_scalar = pltpu.make_async_copy(rows_vector, rows, sems.at[0])
    to_scalar.start()

    v_local = [lax.rem(pairs[0, p], valence.shape[0]) for p in range(n_pairs)]
    c_local = [lax.rem(pairs[1, p], conduction.shape[0]) for p in range(n_pairs)]
    sublane = lax.broadcasted_iota(jnp.int32, (8, LANES), 0)
    gap = jnp.ones((8, LANES), F32)
    for p in range(n_pairs):
        gap = jnp.where(sublane == p, conduction_energy[c_local[p]] - valence_energy[v_local[p]], gap)
    w = -4.0 / (total_pairs * gap)

    def x_stage(chunk, carry):
        lanes = pl.ds(pl.multiple_of(chunk * wide, wide), wide)
        for p in range(n_pairs):
            product = valence[v_local[p], :, lanes] * conduction[c_local[p], :, lanes]
            high, low = split(product)
            spectrum = jnp.dot(
                x_factors[...],
                jnp.concatenate([high, low, high], axis=0),
                preferred_element_type=F32,
            )
            for h in range(2):
                staged[2 * chunk + h, pl.ds(p, EDGE, stride=8), :] = spectrum[:, h * LANES : (h + 1) * LANES]
        return carry

    for n in range(groups):
        for copy in orbitals[n]:
            copy.wait()
        lax.fori_loop(n * span // wide, (n + 1) * span // wide, x_stage, 0)

    first = lax.broadcasted_iota(jnp.int32, (8, LANES), 1) < EDGE

    lower_lanes = lax.broadcasted_iota(jnp.int32, (EDGE, LANES), 1) < EDGE

    def yz_stage(a, carry):
        complex_plane = jnp.where((a & (HALF - 1)) == 0, 0.0, 1.0)
        at_re = pl.ds(pl.multiple_of(a * 8, 8), 8)
        at_im = pl.ds(pl.multiple_of(((a & (HALF - 1)) + HALF) * 8, 8), 8)
        re = [staged[y, at_re, :] for y in range(HALF)]
        im = [staged[y, at_im, :] * complex_plane for y in range(HALF)]
        re, im = small_dft(re, im)
        lower, upper = [], []
        for b in range(HALF):
            r, i = re[b], im[b]
            if b:
                c = y_factors[pl.ds(b, 8, stride=0), :]
                s = y_factors[pl.ds(b + HALF, 8, stride=0), :]
                r, i = r * c - i * s, r * s + i * c
            even = jnp.where(first, r, pltpu.roll(i, EDGE, 1))
            odd = jnp.where(first, pltpu.roll(r, EDGE, 1), i)
            lower.append(even + odd)
            upper.append(even - odd)
        high, low = split(jnp.concatenate(lower + upper, axis=0))
        out = lax.dot_general(
            z_factors[...],
            jnp.concatenate([high, low], axis=1),
            (((1,), (1,)), ((), ())),
            preferred_element_type=F32,
        )
        out = out[: 2 * EDGE] + out[2 * EDGE :]
        for n in range(4):
            re, im = out[:EDGE, n * LANES : (n + 1) * LANES], out[EDGE:, n * LANES : (n + 1) * LANES]
            at = pl.multiple_of((a * 8 + 2 * n) * EDGE, EDGE)
            table[pl.ds(at, EDGE), :] = jnp.where(lower_lanes, re, pltpu.roll(im, EDGE, 1))
            table[pl.ds(at + EDGE, EDGE), :] = jnp.where(lower_lanes, pltpu.roll(re, EDGE, 1), im)
        return carry

    lax.fori_loop(0, HALF + 1, yz_stage, 0)

    to_scalar.wait()
    per_row, per_col = left.shape[2] // LANES, right.shape[2] // LANES

    sublane_bits = [(sublane & (1 << i)) != 0 for i in range(3)]

    def pick(q, picked):
        for j in range(0, LANES, 8):
            some = [table[pl.ds(rows[q, j + t], 8, stride=0), :] for t in range(8)]
            for bit in sublane_bits:
                some = [jnp.where(bit, some[n + 1], some[n]) for n in range(0, len(some), 2)]
            picked[pl.ds(j, 8), :] = some[0]

    def finish(q, picked):
        turned = picked[...].T
        _, b, _, mirrored = half_space(wave[pl.ds(q, 8, stride=0), :])
        bits = [(b & (1 << i)) != 0 for i in range(3)]
        parts = []
        for k in range(2):
            some = [turned[k * EDGE + n * 8 : k * EDGE + n * 8 + 8] for n in range(8)]
            for bit in bits:
                some = [jnp.where(bit, some[n + 1], some[n]) for n in range(0, len(some), 2)]
            parts.append(some[0])
        re, im = parts
        im = jnp.where(mirrored, -im, im)
        plain = jnp.concatenate([re, im], axis=0).astype(BF)
        scaled = jnp.concatenate([w * re, w * im], axis=0).astype(BF)
        at = pl.multiple_of((q % per_row) * LANES, LANES)
        left[q // per_row, :, pl.ds(at, LANES)] = scaled
        at = pl.multiple_of((q % per_col) * LANES, LANES)
        right[q // per_col, :, pl.ds(at, LANES)] = plain

    count = wave.shape[0]
    pick(0, picked_0)

    def select(i, carry):
        pick(2 * i + 1, picked_1)
        finish(2 * i, picked_0)
        pick(jnp.minimum(2 * i + 2, count - 1), picked_0)
        finish(2 * i + 1, picked_1)
        return carry

    lax.fori_loop(0, count // 2, select, 0)


def densities(n_row, n_col, valence, conduction, valence_energy, conduction_energy, pair_list, sphere_index):
    n_pairs, waves = pair_list.shape[0], sphere_index.shape[0]
    tables = [jnp.asarray(x_table()), jnp.asarray(z_table()), jnp.asarray(y_table())]
    hbm = pl.BlockSpec(memory_space=pltpu.HBM)
    vmem = pl.BlockSpec(memory_space=pltpu.VMEM)
    return pl.pallas_call(
        lambda *refs: density_kernel(n_pairs * n_row * n_col, *refs),
        in_specs=[hbm] * 9,
        out_specs=[vmem, vmem],
        out_shape=[
            jax.ShapeDtypeStruct((n_row, 2 * n_pairs, waves // n_row), BF),
            jax.ShapeDtypeStruct((n_col, 2 * n_pairs, waves // n_col), BF),
        ],
        scratch_shapes=[
            pltpu.VMEM((HALF, n_pairs * EDGE, LANES), F32),
            pltpu.VMEM(((HALF + 1) * 8 * EDGE, LANES), F32),
            pltpu.VMEM(valence.shape, F32),
            pltpu.VMEM(conduction.shape, F32),
            pltpu.SMEM(valence_energy.shape, F32),
            pltpu.SMEM(conduction_energy.shape, F32),
            pltpu.SMEM((2, n_pairs), jnp.int32),
            pltpu.VMEM((waves // LANES, LANES), jnp.int32),
            pltpu.VMEM((waves // LANES, LANES), jnp.int32),
            pltpu.SMEM((waves // LANES, LANES), jnp.int32),
            pltpu.VMEM(tables[0].shape, BF),
            pltpu.VMEM(tables[1].shape, BF),
            pltpu.VMEM(tables[2].shape, F32),
            pltpu.VMEM((LANES, LANES), F32),
            pltpu.VMEM((LANES, LANES), F32),
            pltpu.SemaphoreType.DMA((7,)),
            pltpu.SemaphoreType.DMA((2, 4)),
        ],
        compiler_params=pltpu.CompilerParams(vmem_limit_bytes=60 * 1024 * 1024),
        name="density",
    )(
        valence,
        conduction,
        valence_energy,
        conduction_energy,
        pair_list.T,
        sphere_index.reshape(-1, LANES),
        *tables,
    )


def product_kernel(n_left, n_right, *refs):
    left_in, right_in = refs[:n_left], refs[n_left : n_left + n_right]
    out, right, right_sem = refs[n_left + n_right :]

    @pl.when(pl.program_id(0) == 0)
    def _():
        right_slots = right_places(lax.axis_index("row"), lax.axis_index("col") & 1)
        copies = [
            pltpu.make_async_copy(piece, right.at[:, right_slots[j]], right_sem.at[j])
            for j, piece in enumerate(right_in)
        ]
        for copy in copies:
            copy.start()
        for copy in copies:
            copy.wait()

    rows = out.shape[0]
    at = pl.multiple_of(pl.program_id(0) * rows, rows)
    left_slots = left_places(lax.axis_index("col"))
    depth = right.shape[1] * right.shape[2]
    out[...] = lax.dot_general(
        jnp.concatenate([piece[:, :, pl.ds(at, rows)].reshape(depth, rows) for piece in left_in], axis=0),
        jnp.concatenate([right[slot].reshape(depth, right.shape[3]) for slot in left_slots], axis=0),
        (((0,), (0,)), ((), ())),
        preferred_element_type=F32,
    )


def product(left, right):
    n_left, n_right = len(left), len(right)
    rows, cols = left[0].shape[2], right[0].shape[2]
    block = 256
    return pl.pallas_call(
        lambda *refs: product_kernel(n_left, n_right, *refs),
        grid=(rows // block,),
        in_specs=[pl.BlockSpec(memory_space=pltpu.VMEM)] * n_left + [pl.BlockSpec(memory_space=pl.ANY)] * n_right,
        out_specs=pl.BlockSpec((block, cols), lambda m: (m, 0)),
        out_shape=jax.ShapeDtypeStruct((rows, cols), F32),
        scratch_shapes=[
            pltpu.VMEM((right[0].shape[0], n_right) + right[0].shape[1:], BF),
            pltpu.SemaphoreType.DMA((n_right,)),
        ],
        compiler_params=pltpu.CompilerParams(vmem_limit_bytes=24 * 1024 * 1024),
        name="product",
    )(*left, *right)


RING = 4


def shift(value, axis, stride, way):
    n_col, n_row = lax.axis_size("col"), lax.axis_size("row")

    def moved(i, step):
        place = i // stride % RING
        return i + ((place + step) % RING - place) * stride

    pairs = []
    for col in range(n_col):
        for row in range(n_row):
            step = way if col % 2 == 0 else -way
            to = (moved(col, step), row) if axis == "col" else (col, moved(row, step))
            pairs.append((col * n_row + row, to[0] * n_row + to[1]))
    return lax.ppermute(value, ("col", "row"), pairs)


def swap(value, axis, bit):
    count = lax.axis_size(axis)
    return lax.ppermute(value, axis, [(i, i ^ bit) for i in range(count)])


def ring_places(index, stride, core):
    place = lax.rem(lax.div(index, stride), RING)
    base = index - place * stride
    way = 1 - 2 * core
    return [base + lax.rem(place + step, RING) * stride for step in (0, RING - way, RING + way, 2)]


def right_places(row, core):
    return ring_places(row, 1, core) + ring_places(row ^ RING, 1, core)


def left_places(col):
    core = col & 1
    mine = ring_places(col, RING, core) + ring_places(col ^ 2, RING, core)
    theirs = ring_places(col ^ 1, RING, 1 - core) + ring_places(col ^ 3, RING, 1 - core)
    return mine + theirs


def per_device(valence, conduction, valence_energy, conduction_energy, pair_list, sphere_index):
    n_row, n_col = lax.axis_size("row"), lax.axis_size("col")
    left, right = densities(
        n_row, n_col, valence, conduction, valence_energy, conduction_energy, pair_list, sphere_index
    )
    right = lax.all_to_all(right, "col", split_axis=0, concat_axis=0, tiled=True)
    right, left = lax.optimization_barrier((right, left))
    right_z = swap(right, "row", RING)
    rights = [right, shift(right, "row", 1, 1), shift(right, "row", 1, -1)]
    left = lax.all_to_all(left, "row", split_axis=0, concat_axis=0, tiled=True)
    left_z = swap(left, "col", 2)
    lefts = [left, shift(left, "col", RING, 1), shift(left, "col", RING, -1)]
    rights += [shift(rights[1], "row", 1, 1), right_z, shift(right_z, "row", 1, 1), shift(right_z, "row", 1, -1)]
    lefts += [shift(lefts[1], "col", RING, 1)]
    lefts += [left_z, shift(left_z, "col", RING, 1), shift(left_z, "col", RING, -1), swap(lefts[3], "col", 2)]
    rights += [shift(rights[5], "row", 1, 1)]
    lefts += [swap(piece, "col", 1) for piece in lefts]
    return product(lefts, rights)


def solution(mesh):
    return jax.shard_map(
        per_device,
        mesh=mesh,
        in_specs=(
            P("row", None, None),
            P("col", None, None),
            P("row"),
            P("col"),
            P(("col", "row"), None),
            P(),
        ),
        out_specs=P("row", "col"),
        check_vma=False,
    )
```

```python
import math

import jax
import jax.numpy as jnp
import numpy as np
from jax import lax
from jax.experimental import pallas as pl
from jax.experimental.pallas import tpu as pltpu
from jax.sharding import PartitionSpec as P

EDGE = 64
HALF = EDGE // 2
LANES = 128
BF = jnp.bfloat16
F32 = jnp.float32


def two_terms(table):
    high = table.astype(np.float32).astype(BF)
    low = (table - high.astype(np.float64)).astype(BF)
    return np.asarray(high), np.asarray(low)


def x_table():
    x = np.arange(EDGE)
    a = np.arange(HALF)
    angle = 2.0 * np.pi * ((a[:, None] * x[None, :]) % EDGE) / EDGE
    table = np.concatenate([np.cos(angle), -np.sin(angle)], axis=0)
    table[HALF] = 1.0 - 2.0 * (x % 2)
    high, low = two_terms(table)
    return np.concatenate([high, high, low], axis=1)


def z_table():
    z = np.arange(EDGE)
    angle = 2.0 * np.pi * ((z[:, None] * z[None, :]) % EDGE) / EDGE
    cosine, sine = np.cos(angle), np.sin(angle)
    table = np.block([[cosine, sine], [-sine, cosine]]) * EDGE ** (-1.5)
    high, low = two_terms(table)
    return np.block([[high, high], [low, np.zeros_like(low)]]).astype(BF)


def y_table():
    angle = 2.0 * np.pi * np.arange(HALF) / EDGE
    odd = np.arange(LANES)[None, :] >= EDGE
    real = np.where(odd, np.cos(angle)[:, None], 1.0)
    imag = np.where(odd, -np.sin(angle)[:, None], 0.0)
    return np.concatenate([real, imag], axis=0).astype(np.float32)


def small_dft(re, im):
    n = len(re)
    if n == 1:
        return re, im
    even_re, even_im = small_dft(re[0::2], im[0::2])
    odd_re, odd_im = small_dft(re[1::2], im[1::2])
    out_re, out_im = [None] * n, [None] * n
    for k in range(n // 2):
        r, i = odd_re[k], odd_im[k]
        if k == 0:
            pass
        elif 4 * k == n:
            r, i = i, -r
        elif 8 * k == n:
            s = math.sqrt(0.5)
            r, i = (r + i) * s, (i - r) * s
        elif 8 * k == 3 * n:
            s = math.sqrt(0.5)
            r, i = (i - r) * s, (r + i) * -s
        else:
            c, s = math.cos(2 * math.pi * k / n), math.sin(2 * math.pi * k / n)
            r, i = r * c + i * s, i * c - r * s
        out_re[k], out_im[k] = even_re[k] + r, even_im[k] + i
        out_re[k + n // 2], out_im[k + n // 2] = even_re[k] - r, even_im[k] - i
    return out_re, out_im


def split(value):
    high = value.astype(BF)
    return high, (value - high.astype(F32)).astype(BF)


def half_space(index):
    a, b, c = index >> 12, (index >> 6) & (EDGE - 1), index & (EDGE - 1)
    mirrored = a > HALF
    a = jnp.where(mirrored, EDGE - a, a)
    b = jnp.where(mirrored, (EDGE - b) & (EDGE - 1), b)
    c = jnp.where(mirrored, (EDGE - c) & (EDGE - 1), c)
    return a, b, c, mirrored


def density_kernel(
    total_pairs,
    valence_hbm,
    conduction_hbm,
    valence_energy_hbm,
    conduction_energy_hbm,
    pairs_hbm,
    wave_hbm,
    x_factors_hbm,
    z_factors_hbm,
    y_factors_hbm,
    left,
    right,
    staged,
    table,
    valence,
    conduction,
    valence_energy,
    conduction_energy,
    pairs,
    wave,
    rows_vector,
    rows,
    x_factors,
    z_factors,
    y_factors,
    picked_0,
    picked_1,
    sems,
    orbital_sems,
):
    n_pairs = 8
    wide = 2 * LANES
    groups = orbital_sems.shape[1]
    span = EDGE * EDGE // groups

    small = [
        pltpu.make_async_copy(src, dst, sems.at[i])
        for i, (src, dst) in enumerate(
            [
                (pairs_hbm, pairs),
                (x_factors_hbm, x_factors),
                (wave_hbm, wave),
                (valence_energy_hbm, valence_energy),
                (conduction_energy_hbm, conduction_energy),
                (z_factors_hbm, z_factors),
                (y_factors_hbm, y_factors),
            ]
        )
    ]
    for copy in small:
        copy.start()
    orbitals = []
    for n in range(groups):
        at = pl.ds(n * span, span)
        orbitals.append(
            [
                pltpu.make_async_copy(valence_hbm.at[:, :, at], valence.at[:, :, at], orbital_sems.at[0, n]),
                pltpu.make_async_copy(conduction_hbm.at[:, :, at], conduction.at[:, :, at], orbital_sems.at[1, n]),
            ]
        )
        for copy in orbitals[-1]:
            copy.start()
    for copy in small:
        copy.wait()

    a, b, c, _ = half_space(wave[...])
    rows_vector[...] = (a * 8 + (b >> 3)) * EDGE + c
    to_scalar = pltpu.make_async_copy(rows_vector, rows, sems.at[0])
    to_scalar.start()

    v_local = [lax.rem(pairs[0, p], valence.shape[0]) for p in range(n_pairs)]
    c_local = [lax.rem(pairs[1, p], conduction.shape[0]) for p in range(n_pairs)]
    sublane = lax.broadcasted_iota(jnp.int32, (8, LANES), 0)
    gap = jnp.ones((8, LANES), F32)
    for p in range(n_pairs):
        gap = jnp.where(sublane == p, conduction_energy[c_local[p]] - valence_energy[v_local[p]], gap)
    w = -4.0 / (total_pairs * gap)

    def x_stage(chunk, carry):
        lanes = pl.ds(pl.multiple_of(chunk * wide, wide), wide)
        for p in range(n_pairs):
            product = valence[v_local[p], :, lanes] * conduction[c_local[p], :, lanes]
            high, low = split(product)
            spectrum = jnp.dot(
                x_factors[...],
                jnp.concatenate([high, low, high], axis=0),
                preferred_element_type=F32,
            )
            for h in range(2):
                staged[2 * chunk + h, pl.ds(p, EDGE, stride=8), :] = spectrum[:, h * LANES : (h + 1) * LANES]
        return carry

    for n in range(groups):
        for copy in orbitals[n]:
            copy.wait()
        lax.fori_loop(n * span // wide, (n + 1) * span // wide, x_stage, 0, unroll=4)

    first = lax.broadcasted_iota(jnp.int32, (8, LANES), 1) < EDGE

    lower_lanes = lax.broadcasted_iota(jnp.int32, (EDGE, LANES), 1) < EDGE

    def yz_stage(a, carry):
        complex_plane = jnp.where((a & (HALF - 1)) == 0, 0.0, 1.0)
        at_re = pl.ds(pl.multiple_of(a * 8, 8), 8)
        at_im = pl.ds(pl.multiple_of(((a & (HALF - 1)) + HALF) * 8, 8), 8)
        re = [staged[y, at_re, :] for y in range(HALF)]
        im = [staged[y, at_im, :] * complex_plane for y in range(HALF)]
        re, im = small_dft(re, im)
        lower, upper = [], []
        for b in range(HALF):
            r, i = re[b], im[b]
            if b:
                c = y_factors[pl.ds(b, 8, stride=0), :]
                s = y_factors[pl.ds(b + HALF, 8, stride=0), :]
                r, i = r * c - i * s, r * s + i * c
            even = jnp.where(first, r, pltpu.roll(i, EDGE, 1))
            odd = jnp.where(first, pltpu.roll(r, EDGE, 1), i)
            lower.append(even + odd)
            upper.append(even - odd)
        high, low = split(jnp.concatenate(lower + upper, axis=0))
        out = lax.dot_general(
            z_factors[...],
            jnp.concatenate([high, low], axis=1),
            (((1,), (1,)), ((), ())),
            preferred_element_type=F32,
        )
        out = out[: 2 * EDGE] + out[2 * EDGE :]
        for n in range(4):
            re, im = out[:EDGE, n * LANES : (n + 1) * LANES], out[EDGE:, n * LANES : (n + 1) * LANES]
            at = pl.multiple_of((a * 8 + 2 * n) * EDGE, EDGE)
            table[pl.ds(at, EDGE), :] = jnp.where(lower_lanes, re, pltpu.roll(im, EDGE, 1))
            table[pl.ds(at + EDGE, EDGE), :] = jnp.where(lower_lanes, pltpu.roll(re, EDGE, 1), im)
        return carry

    lax.fori_loop(0, HALF + 1, yz_stage, 0, unroll=3)

    to_scalar.wait()
    per_row, per_col = left.shape[2] // LANES, right.shape[2] // LANES

    sublane_bits = [(sublane & (1 << i)) != 0 for i in range(3)]

    def pick(q, picked):
        line = rows.at[q]
        for j in range(0, LANES, 8):
            some = [table[pl.ds(line[j + t], 8, stride=0), :] for t in range(8)]
            for bit in sublane_bits:
                some = [jnp.where(bit, some[n + 1], some[n]) for n in range(0, len(some), 2)]
            picked[pl.ds(j, 8), :] = some[0]

    def finish(q, picked):
        turned = picked[...].T
        _, b, _, mirrored = half_space(wave[pl.ds(q, 8, stride=0), :])
        bits = [(b & (1 << i)) != 0 for i in range(3)]
        parts = []
        for k in range(2):
            some = [turned[k * EDGE + n * 8 : k * EDGE + n * 8 + 8] for n in range(8)]
            for bit in bits:
                some = [jnp.where(bit, some[n + 1], some[n]) for n in range(0, len(some), 2)]
            parts.append(some[0])
        re, im = parts
        im = jnp.where(mirrored, -im, im)
        plain = jnp.concatenate([re, im], axis=0).astype(BF)
        scaled = jnp.concatenate([w * re, w * im], axis=0).astype(BF)
        at = pl.multiple_of((q % per_row) * LANES, LANES)
        left[q // per_row, :, pl.ds(at, LANES)] = scaled
        at = pl.multiple_of((q % per_col) * LANES, LANES)
        right[q // per_col, :, pl.ds(at, LANES)] = plain

    count = wave.shape[0]
    pick(0, picked_0)

    def select(i, carry):
        pick(2 * i + 1, picked_1)
        finish(2 * i, picked_0)
        pick(jnp.minimum(2 * i + 2, count - 1), picked_0)
        finish(2 * i + 1, picked_1)
        return carry

    lax.fori_loop(0, count // 2, select, 0, unroll=8)


def densities(n_row, n_col, valence, conduction, valence_energy, conduction_energy, pair_list, sphere_index):
    n_pairs, waves = pair_list.shape[0], sphere_index.shape[0]
    tables = [jnp.asarray(x_table()), jnp.asarray(z_table()), jnp.asarray(y_table())]
    hbm = pl.BlockSpec(memory_space=pltpu.HBM)
    vmem = pl.BlockSpec(memory_space=pltpu.VMEM)
    return pl.pallas_call(
        lambda *refs: density_kernel(n_pairs * n_row * n_col, *refs),
        in_specs=[hbm] * 9,
        out_specs=[vmem, vmem],
        out_shape=[
            jax.ShapeDtypeStruct((n_row, 2 * n_pairs, waves // n_row), BF),
            jax.ShapeDtypeStruct((n_col, 2 * n_pairs, waves // n_col), BF),
        ],
        scratch_shapes=[
            pltpu.VMEM((HALF, n_pairs * EDGE, LANES), F32),
            pltpu.VMEM(((HALF + 1) * 8 * EDGE, LANES), F32),
            pltpu.VMEM(valence.shape, F32),
            pltpu.VMEM(conduction.shape, F32),
            pltpu.SMEM(valence_energy.shape, F32),
            pltpu.SMEM(conduction_energy.shape, F32),
            pltpu.SMEM((2, n_pairs), jnp.int32),
            pltpu.VMEM((waves // LANES, LANES), jnp.int32),
            pltpu.VMEM((waves // LANES, LANES), jnp.int32),
            pltpu.SMEM((waves // LANES, LANES), jnp.int32),
            pltpu.VMEM(tables[0].shape, BF),
            pltpu.VMEM(tables[1].shape, BF),
            pltpu.VMEM(tables[2].shape, F32),
            pltpu.VMEM((LANES, LANES), F32),
            pltpu.VMEM((LANES, LANES), F32),
            pltpu.SemaphoreType.DMA((7,)),
            pltpu.SemaphoreType.DMA((2, 4)),
        ],
        compiler_params=pltpu.CompilerParams(vmem_limit_bytes=60 * 1024 * 1024),
        name="density",
    )(
        valence,
        conduction,
        valence_energy,
        conduction_energy,
        pair_list.T,
        sphere_index.reshape(-1, LANES),
        *tables,
    )


def product_kernel(n_left, n_right, *refs):
    left_in, right_in = refs[:n_left], refs[n_left : n_left + n_right]
    out, right, right_sem = refs[n_left + n_right :]

    @pl.when(pl.program_id(0) == 0)
    def _():
        right_slots = right_places(lax.axis_index("row"), lax.axis_index("col") & 1)
        copies = [
            pltpu.make_async_copy(piece, right.at[:, right_slots[j]], right_sem.at[j])
            for j, piece in enumerate(right_in)
        ]
        for copy in copies:
            copy.start()
        for copy in copies:
            copy.wait()

    rows = out.shape[0]
    at = pl.multiple_of(pl.program_id(0) * rows, rows)
    left_slots = left_places(lax.axis_index("col"))
    depth = right.shape[1] * right.shape[2]
    out[...] = lax.dot_general(
        jnp.concatenate([piece[:, :, pl.ds(at, rows)].reshape(depth, rows) for piece in left_in], axis=0),
        jnp.concatenate([right[slot].reshape(depth, right.shape[3]) for slot in left_slots], axis=0),
        (((0,), (0,)), ((), ())),
        preferred_element_type=F32,
    )


def product(left, right):
    n_left, n_right = len(left), len(right)
    rows, cols = left[0].shape[2], right[0].shape[2]
    block = 256
    return pl.pallas_call(
        lambda *refs: product_kernel(n_left, n_right, *refs),
        grid=(rows // block,),
        in_specs=[pl.BlockSpec(memory_space=pltpu.VMEM)] * n_left + [pl.BlockSpec(memory_space=pl.ANY)] * n_right,
        out_specs=pl.BlockSpec((block, cols), lambda m: (m, 0)),
        out_shape=jax.ShapeDtypeStruct((rows, cols), F32),
        scratch_shapes=[
            pltpu.VMEM((right[0].shape[0], n_right) + right[0].shape[1:], BF),
            pltpu.SemaphoreType.DMA((n_right,)),
        ],
        compiler_params=pltpu.CompilerParams(vmem_limit_bytes=24 * 1024 * 1024),
        name="product",
    )(*left, *right)


RING = 4


def shift(value, axis, stride, way):
    n_col, n_row = lax.axis_size("col"), lax.axis_size("row")

    def moved(i, step):
        place = i // stride % RING
        return i + ((place + step) % RING - place) * stride

    pairs = []
    for col in range(n_col):
        for row in range(n_row):
            step = way if col % 2 == 0 else -way
            to = (moved(col, step), row) if axis == "col" else (col, moved(row, step))
            pairs.append((col * n_row + row, to[0] * n_row + to[1]))
    return lax.ppermute(value, ("col", "row"), pairs)


def swap(value, axis, bit):
    count = lax.axis_size(axis)
    return lax.ppermute(value, axis, [(i, i ^ bit) for i in range(count)])


def ring_places(index, stride, core):
    place = lax.rem(lax.div(index, stride), RING)
    base = index - place * stride
    way = 1 - 2 * core
    return [base + lax.rem(place + step, RING) * stride for step in (0, RING - way, RING + way, 2)]


def right_places(row, core):
    return ring_places(row, 1, core) + ring_places(row ^ RING, 1, core)


def left_places(col):
    core = col & 1
    mine = ring_places(col, RING, core) + ring_places(col ^ 2, RING, core)
    theirs = ring_places(col ^ 1, RING, 1 - core) + ring_places(col ^ 3, RING, 1 - core)
    return mine + theirs


def per_device(valence, conduction, valence_energy, conduction_energy, pair_list, sphere_index):
    n_row, n_col = lax.axis_size("row"), lax.axis_size("col")
    left, right = densities(
        n_row, n_col, valence, conduction, valence_energy, conduction_energy, pair_list, sphere_index
    )
    right = lax.all_to_all(right, "col", split_axis=0, concat_axis=0, tiled=True)
    right, left = lax.optimization_barrier((right, left))
    right_z = swap(right, "row", RING)
    rights = [right, shift(right, "row", 1, 1), shift(right, "row", 1, -1)]
    left = lax.all_to_all(left, "row", split_axis=0, concat_axis=0, tiled=True)
    left_z = swap(left, "col", 2)
    lefts = [left, shift(left, "col", RING, 1), shift(left, "col", RING, -1)]
    rights += [shift(rights[1], "row", 1, 1), right_z, shift(right_z, "row", 1, 1), shift(right_z, "row", 1, -1)]
    lefts += [shift(lefts[1], "col", RING, 1)]
    lefts += [left_z, shift(left_z, "col", RING, 1), shift(left_z, "col", RING, -1), swap(lefts[3], "col", 2)]
    rights += [shift(rights[5], "row", 1, 1)]
    lefts += [swap(piece, "col", 1) for piece in lefts]
    return product(lefts, rights)


def solution(mesh):
    return jax.shard_map(
        per_device,
        mesh=mesh,
        in_specs=(
            P("row", None, None),
            P("col", None, None),
            P("row"),
            P("col"),
            P(("col", "row"), None),
            P(),
        ),
        out_specs=P("row", "col"),
        check_vma=False,
    )
```

```python
import math

import jax
import jax.numpy as jnp
import numpy as np
from jax import lax
from jax.experimental import pallas as pl
from jax.experimental.pallas import tpu as pltpu
from jax.sharding import PartitionSpec as P

EDGE = 64
HALF = EDGE // 2
LANES = 128
BF = jnp.bfloat16
F32 = jnp.float32


def two_terms(table):
    high = table.astype(np.float32).astype(BF)
    low = (table - high.astype(np.float64)).astype(BF)
    return np.asarray(high), np.asarray(low)


def x_table():
    x = np.arange(EDGE)
    a = np.arange(HALF)
    angle = 2.0 * np.pi * ((a[:, None] * x[None, :]) % EDGE) / EDGE
    table = np.concatenate([np.cos(angle), -np.sin(angle)], axis=0)
    table[HALF] = 1.0 - 2.0 * (x % 2)
    high, low = two_terms(table)
    return np.concatenate([high, high, low], axis=1)


def z_table():
    z = np.arange(EDGE)
    angle = 2.0 * np.pi * ((z[:, None] * z[None, :]) % EDGE) / EDGE
    cosine, sine = np.cos(angle), np.sin(angle)
    table = np.block([[cosine, sine], [-sine, cosine]]) * EDGE ** (-1.5)
    high, low = two_terms(table)
    return np.block([[high, high], [low, np.zeros_like(low)]]).astype(BF)


def y_table():
    angle = 2.0 * np.pi * np.arange(HALF) / EDGE
    odd = np.arange(LANES)[None, :] >= EDGE
    real = np.where(odd, np.cos(angle)[:, None], 1.0)
    imag = np.where(odd, -np.sin(angle)[:, None], 0.0)
    return np.concatenate([real, imag], axis=0).astype(np.float32)


def small_dft(re, im):
    n = len(re)
    if n == 1:
        return re, im
    even_re, even_im = small_dft(re[0::2], im[0::2])
    odd_re, odd_im = small_dft(re[1::2], im[1::2])
    out_re, out_im = [None] * n, [None] * n
    for k in range(n // 2):
        r, i = odd_re[k], odd_im[k]
        if k == 0:
            pass
        elif 4 * k == n:
            r, i = i, -r
        elif 8 * k == n:
            s = math.sqrt(0.5)
            r, i = (r + i) * s, (i - r) * s
        elif 8 * k == 3 * n:
            s = math.sqrt(0.5)
            r, i = (i - r) * s, (r + i) * -s
        else:
            c, s = math.cos(2 * math.pi * k / n), math.sin(2 * math.pi * k / n)
            r, i = r * c + i * s, i * c - r * s
        out_re[k], out_im[k] = even_re[k] + r, even_im[k] + i
        out_re[k + n // 2], out_im[k + n // 2] = even_re[k] - r, even_im[k] - i
    return out_re, out_im


def split(value):
    high = value.astype(BF)
    return high, (value - high.astype(F32)).astype(BF)


def half_space(index):
    a, b, c = index >> 12, (index >> 6) & (EDGE - 1), index & (EDGE - 1)
    mirrored = a > HALF
    a = jnp.where(mirrored, EDGE - a, a)
    b = jnp.where(mirrored, (EDGE - b) & (EDGE - 1), b)
    c = jnp.where(mirrored, (EDGE - c) & (EDGE - 1), c)
    return a, b, c, mirrored


def density_kernel(
    total_pairs,
    valence_hbm,
    conduction_hbm,
    valence_energy_hbm,
    conduction_energy_hbm,
    pairs_hbm,
    wave_hbm,
    x_factors_hbm,
    z_factors_hbm,
    y_factors_hbm,
    left,
    right,
    staged,
    table,
    valence,
    conduction,
    valence_energy,
    conduction_energy,
    pairs,
    wave,
    rows_vector,
    rows,
    x_factors,
    z_factors,
    y_factors,
    picked_0,
    picked_1,
    sems,
    orbital_sems,
):
    n_pairs = 8
    wide = 2 * LANES
    groups = orbital_sems.shape[1]
    span = EDGE * EDGE // groups

    small = [
        pltpu.make_async_copy(src, dst, sems.at[i])
        for i, (src, dst) in enumerate(
            [
                (pairs_hbm, pairs),
                (x_factors_hbm, x_factors),
                (wave_hbm, wave),
                (valence_energy_hbm, valence_energy),
                (conduction_energy_hbm, conduction_energy),
                (z_factors_hbm, z_factors),
                (y_factors_hbm, y_factors),
            ]
        )
    ]
    for copy in small:
        copy.start()
    orbitals = []
    for n in range(groups):
        at = pl.ds(n * span, span)
        orbitals.append(
            [
                pltpu.make_async_copy(valence_hbm.at[:, :, at], valence.at[:, :, at], orbital_sems.at[0, n]),
                pltpu.make_async_copy(conduction_hbm.at[:, :, at], conduction.at[:, :, at], orbital_sems.at[1, n]),
            ]
        )
        for copy in orbitals[-1]:
            copy.start()
    for copy in small:
        copy.wait()

    a, b, c, _ = half_space(wave[...])
    rows_vector[...] = (a * 8 + (b >> 3)) * EDGE + c
    to_scalar = pltpu.make_async_copy(rows_vector, rows, sems.at[0])
    to_scalar.start()

    v_local = [lax.rem(pairs[0, p], valence.shape[0]) for p in range(n_pairs)]
    c_local = [lax.rem(pairs[1, p], conduction.shape[0]) for p in range(n_pairs)]
    sublane = lax.broadcasted_iota(jnp.int32, (8, LANES), 0)
    gap = jnp.ones((8, LANES), F32)
    for p in range(n_pairs):
        gap = jnp.where(sublane == p, conduction_energy[c_local[p]] - valence_energy[v_local[p]], gap)
    w = -4.0 / (total_pairs * gap)

    def x_stage(chunk, carry):
        lanes = pl.ds(pl.multiple_of(chunk * wide, wide), wide)
        for p in range(n_pairs):
            product = valence[v_local[p], :, lanes] * conduction[c_local[p], :, lanes]
            high, low = split(product)
            spectrum = jnp.dot(
                x_factors[...],
                jnp.concatenate([high, low, high], axis=0),
                preferred_element_type=F32,
            )
            for h in range(2):
                staged[2 * chunk + h, pl.ds(p, EDGE, stride=8), :] = spectrum[:, h * LANES : (h + 1) * LANES]
        return carry

    for n in range(groups):
        for copy in orbitals[n]:
            copy.wait()
        lax.fori_loop(n * span // wide, (n + 1) * span // wide, x_stage, 0, unroll=4)

    first = lax.broadcasted_iota(jnp.int32, (8, LANES), 1) < EDGE

    lower_lanes = lax.broadcasted_iota(jnp.int32, (EDGE, LANES), 1) < EDGE

    def yz_stage(a, carry):
        complex_plane = jnp.where((a & (HALF - 1)) == 0, 0.0, 1.0)
        at_re = pl.ds(pl.multiple_of(a * 8, 8), 8)
        at_im = pl.ds(pl.multiple_of(((a & (HALF - 1)) + HALF) * 8, 8), 8)
        re = [staged[y, at_re, :] for y in range(HALF)]
        im = [staged[y, at_im, :] * complex_plane for y in range(HALF)]
        re, im = small_dft(re, im)
        lower, upper = [], []
        for b in range(HALF):
            r, i = re[b], im[b]
            if b:
                c = y_factors[pl.ds(b, 8, stride=0), :]
                s = y_factors[pl.ds(b + HALF, 8, stride=0), :]
                r, i = r * c - i * s, r * s + i * c
            even = jnp.where(first, r, pltpu.roll(i, EDGE, 1))
            odd = jnp.where(first, pltpu.roll(r, EDGE, 1), i)
            lower.append(even + odd)
            upper.append(even - odd)
        high, low = split(jnp.concatenate(lower + upper, axis=0))
        out = lax.dot_general(
            z_factors[...],
            jnp.concatenate([high, low], axis=1),
            (((1,), (1,)), ((), ())),
            preferred_element_type=F32,
        )
        out = out[: 2 * EDGE] + out[2 * EDGE :]
        for n in range(4):
            re, im = out[:EDGE, n * LANES : (n + 1) * LANES], out[EDGE:, n * LANES : (n + 1) * LANES]
            at = pl.multiple_of((a * 8 + 2 * n) * EDGE, EDGE)
            table[pl.ds(at, EDGE), :] = jnp.where(lower_lanes, re, pltpu.roll(im, EDGE, 1))
            table[pl.ds(at + EDGE, EDGE), :] = jnp.where(lower_lanes, pltpu.roll(re, EDGE, 1), im)
        return carry

    lax.fori_loop(0, HALF + 1, yz_stage, 0, unroll=3)

    to_scalar.wait()
    per_row, per_col = left.shape[2] // LANES, right.shape[2] // LANES

    sublane_bits = [(sublane & (1 << i)) != 0 for i in range(3)]

    def pick(q, picked):
        line = rows.at[q]
        for j in range(0, LANES, 8):
            some = [table[pl.ds(line[j + t], 8, stride=0), :] for t in range(8)]
            for bit in sublane_bits:
                some = [jnp.where(bit, some[n + 1], some[n]) for n in range(0, len(some), 2)]
            picked[pl.ds(j, 8), :] = some[0]

    def finish(q, picked):
        turned = picked[...].T
        _, b, _, mirrored = half_space(wave[pl.ds(q, 8, stride=0), :])
        bits = [(b & (1 << i)) != 0 for i in range(3)]
        parts = []
        for k in range(2):
            some = [turned[k * EDGE + n * 8 : k * EDGE + n * 8 + 8] for n in range(8)]
            for bit in bits:
                some = [jnp.where(bit, some[n + 1], some[n]) for n in range(0, len(some), 2)]
            parts.append(some[0])
        re, im = parts
        im = jnp.where(mirrored, -im, im)
        plain = jnp.concatenate([re, im], axis=0).astype(BF)
        scaled = jnp.concatenate([w * re, w * im], axis=0).astype(BF)
        at = pl.multiple_of((q % per_row) * LANES, LANES)
        left[q // per_row, :, pl.ds(at, LANES)] = scaled
        at = pl.multiple_of((q % per_col) * LANES, LANES)
        right[q // per_col, :, pl.ds(at, LANES)] = plain

    count = wave.shape[0]
    pick(0, picked_0)

    def select(i, carry):
        pick(2 * i + 1, picked_1)
        finish(2 * i, picked_0)
        pick(jnp.minimum(2 * i + 2, count - 1), picked_0)
        finish(2 * i + 1, picked_1)
        return carry

    lax.fori_loop(0, count // 2, select, 0, unroll=8)


def densities(n_row, n_col, valence, conduction, valence_energy, conduction_energy, pair_list, sphere_index):
    n_pairs, waves = pair_list.shape[0], sphere_index.shape[0]
    tables = [jnp.asarray(x_table()), jnp.asarray(z_table()), jnp.asarray(y_table())]
    hbm = pl.BlockSpec(memory_space=pltpu.HBM)
    vmem = pl.BlockSpec(memory_space=pltpu.VMEM)
    return pl.pallas_call(
        lambda *refs: density_kernel(n_pairs * n_row * n_col, *refs),
        in_specs=[hbm] * 9,
        out_specs=[vmem, vmem],
        out_shape=[
            jax.ShapeDtypeStruct((n_row, 2 * n_pairs, waves // n_row), BF),
            jax.ShapeDtypeStruct((n_col, 2 * n_pairs, waves // n_col), BF),
        ],
        scratch_shapes=[
            pltpu.VMEM((HALF, n_pairs * EDGE, LANES), F32),
            pltpu.VMEM(((HALF + 1) * 8 * EDGE, LANES), F32),
            pltpu.VMEM(valence.shape, F32),
            pltpu.VMEM(conduction.shape, F32),
            pltpu.SMEM(valence_energy.shape, F32),
            pltpu.SMEM(conduction_energy.shape, F32),
            pltpu.SMEM((2, n_pairs), jnp.int32),
            pltpu.VMEM((waves // LANES, LANES), jnp.int32),
            pltpu.VMEM((waves // LANES, LANES), jnp.int32),
            pltpu.SMEM((waves // LANES, LANES), jnp.int32),
            pltpu.VMEM(tables[0].shape, BF),
            pltpu.VMEM(tables[1].shape, BF),
            pltpu.VMEM(tables[2].shape, F32),
            pltpu.VMEM((LANES, LANES), F32),
            pltpu.VMEM((LANES, LANES), F32),
            pltpu.SemaphoreType.DMA((7,)),
            pltpu.SemaphoreType.DMA((2, 4)),
        ],
        compiler_params=pltpu.CompilerParams(vmem_limit_bytes=60 * 1024 * 1024),
        name="density",
    )(
        valence,
        conduction,
        valence_energy,
        conduction_energy,
        pair_list.T,
        sphere_index.reshape(-1, LANES),
        *tables,
    )


def product_kernel(n_left, n_right, *refs):
    left, right, out = refs[:n_left], refs[n_left : n_left + n_right], refs[n_left + n_right]
    col, row = lax.axis_index("col"), lax.axis_index("row")
    left_slots, right_slots = left_places(col), right_places(row, col & 1)
    rows = out.shape[0]
    at = pl.multiple_of(pl.program_id(0) * rows, rows)
    out[...] = lax.dot_general(
        jnp.concatenate([piece[slot, :, pl.ds(at, rows)] for slot in right_slots for piece in left], axis=0),
        jnp.concatenate([piece[slot] for piece in right for slot in left_slots], axis=0),
        (((0,), (0,)), ((), ())),
        preferred_element_type=F32,
    )


def product(left, right):
    n_left, n_right = len(left), len(right)
    rows, cols = left[0].shape[2], right[0].shape[2]
    block = 512
    return pl.pallas_call(
        lambda *refs: product_kernel(n_left, n_right, *refs),
        grid=(rows // block,),
        in_specs=[pl.BlockSpec(memory_space=pltpu.VMEM)] * (n_left + n_right),
        out_specs=pl.BlockSpec((block, cols), lambda m: (m, 0)),
        out_shape=jax.ShapeDtypeStruct((rows, cols), F32),
        compiler_params=pltpu.CompilerParams(vmem_limit_bytes=32 * 1024 * 1024),
        name="product",
    )(*left, *right)


RING = 4


def shift(value, axis, stride, way):
    n_col, n_row = lax.axis_size("col"), lax.axis_size("row")

    def moved(i, step):
        place = i // stride % RING
        return i + ((place + step) % RING - place) * stride

    pairs = []
    for col in range(n_col):
        for row in range(n_row):
            step = way if col % 2 == 0 else -way
            to = (moved(col, step), row) if axis == "col" else (col, moved(row, step))
            pairs.append((col * n_row + row, to[0] * n_row + to[1]))
    return lax.ppermute(value, ("col", "row"), pairs)


def swap(value, axis, bit):
    count = lax.axis_size(axis)
    return lax.ppermute(value, axis, [(i, i ^ bit) for i in range(count)])


def ring_places(index, stride, core):
    place = lax.rem(lax.div(index, stride), RING)
    base = index - place * stride
    way = 1 - 2 * core
    return [base + lax.rem(place + step, RING) * stride for step in (0, RING - way, RING + way, 2)]


def right_places(row, core):
    return ring_places(row, 1, core) + ring_places(row ^ RING, 1, core)


def left_places(col):
    core = col & 1
    mine = ring_places(col, RING, core) + ring_places(col ^ 2, RING, core)
    theirs = ring_places(col ^ 1, RING, 1 - core) + ring_places(col ^ 3, RING, 1 - core)
    return mine + theirs


def per_device(valence, conduction, valence_energy, conduction_energy, pair_list, sphere_index):
    n_row, n_col = lax.axis_size("row"), lax.axis_size("col")
    left, right = densities(
        n_row, n_col, valence, conduction, valence_energy, conduction_energy, pair_list, sphere_index
    )
    right = lax.all_to_all(right, "col", split_axis=0, concat_axis=0, tiled=True)
    right, left = lax.optimization_barrier((right, left))
    right_z = swap(right, "row", RING)
    rights = [right, shift(right, "row", 1, 1), shift(right, "row", 1, -1)]
    left = lax.all_to_all(left, "row", split_axis=0, concat_axis=0, tiled=True)
    left_z = swap(left, "col", 2)
    lefts = [left, shift(left, "col", RING, 1), shift(left, "col", RING, -1)]
    rights += [shift(rights[1], "row", 1, 1), right_z, shift(right_z, "row", 1, 1), shift(right_z, "row", 1, -1)]
    lefts += [shift(lefts[1], "col", RING, 1)]
    lefts += [left_z, shift(left_z, "col", RING, 1), shift(left_z, "col", RING, -1), swap(lefts[3], "col", 2)]
    rights += [shift(rights[5], "row", 1, 1)]
    lefts += [swap(piece, "col", 1) for piece in lefts]
    return product(lefts, rights)


def solution(mesh):
    return jax.shard_map(
        per_device,
        mesh=mesh,
        in_specs=(
            P("row", None, None),
            P("col", None, None),
            P("row"),
            P("col"),
            P(("col", "row"), None),
            P(),
        ),
        out_specs=P("row", "col"),
        check_vma=False,
    )
```

```python
import math

import jax
import jax.numpy as jnp
import numpy as np
from jax import lax
from jax.experimental import pallas as pl
from jax.experimental.pallas import tpu as pltpu
from jax.sharding import PartitionSpec as P

EDGE = 64
HALF = EDGE // 2
LANES = 128
BF = jnp.bfloat16
F32 = jnp.float32


def two_terms(table):
    high = table.astype(np.float32).astype(BF)
    low = (table - high.astype(np.float64)).astype(BF)
    return np.asarray(high), np.asarray(low)


def x_table():
    x = np.arange(EDGE)
    a = np.arange(HALF)
    angle = 2.0 * np.pi * ((a[:, None] * x[None, :]) % EDGE) / EDGE
    table = np.concatenate([np.cos(angle), -np.sin(angle)], axis=0)
    table[HALF] = 1.0 - 2.0 * (x % 2)
    high, low = two_terms(table)
    return np.block([[high, high], [low, np.zeros_like(low)]]).astype(BF)


def z_table():
    z = np.arange(EDGE)
    angle = 2.0 * np.pi * ((z[:, None] * z[None, :]) % EDGE) / EDGE
    cosine, sine = np.cos(angle), np.sin(angle)
    table = np.block([[cosine, sine], [-sine, cosine]]) * EDGE ** (-1.5)
    high, low = two_terms(table)
    return np.block([[high, high], [low, np.zeros_like(low)]]).astype(BF)


def y_table():
    angle = 2.0 * np.pi * np.arange(HALF) / EDGE
    odd = np.arange(LANES)[None, :] >= EDGE
    real = np.where(odd, np.cos(angle)[:, None], 1.0)
    imag = np.where(odd, -np.sin(angle)[:, None], 0.0)
    return np.concatenate([real, imag], axis=0).astype(np.float32)


def small_dft(re, im):
    n = len(re)
    if n == 1:
        return re, im
    even_re, even_im = small_dft(re[0::2], im[0::2])
    odd_re, odd_im = small_dft(re[1::2], im[1::2])
    out_re, out_im = [None] * n, [None] * n
    for k in range(n // 2):
        r, i = odd_re[k], odd_im[k]
        if k == 0:
            pass
        elif 4 * k == n:
            r, i = i, -r
        elif 8 * k == n:
            s = math.sqrt(0.5)
            r, i = (r + i) * s, (i - r) * s
        elif 8 * k == 3 * n:
            s = math.sqrt(0.5)
            r, i = (i - r) * s, (r + i) * -s
        else:
            c, s = math.cos(2 * math.pi * k / n), math.sin(2 * math.pi * k / n)
            r, i = r * c + i * s, i * c - r * s
        out_re[k], out_im[k] = even_re[k] + r, even_im[k] + i
        out_re[k + n // 2], out_im[k + n // 2] = even_re[k] - r, even_im[k] - i
    return out_re, out_im


def split(value):
    high = value.astype(BF)
    return high, (value - high.astype(F32)).astype(BF)


def half_space(index):
    a, b, c = index >> 12, (index >> 6) & (EDGE - 1), index & (EDGE - 1)
    mirrored = a > HALF
    a = jnp.where(mirrored, EDGE - a, a)
    b = jnp.where(mirrored, (EDGE - b) & (EDGE - 1), b)
    c = jnp.where(mirrored, (EDGE - c) & (EDGE - 1), c)
    return a, b, c, mirrored


def density_kernel(
    total_pairs,
    valence_hbm,
    conduction_hbm,
    valence_energy_hbm,
    conduction_energy_hbm,
    pairs_hbm,
    wave_hbm,
    x_factors_hbm,
    z_factors_hbm,
    y_factors_hbm,
    left,
    right,
    staged,
    table,
    valence,
    conduction,
    valence_energy,
    conduction_energy,
    pairs,
    wave,
    rows_vector,
    rows,
    x_factors,
    z_factors,
    y_factors,
    picked_0,
    picked_1,
    sems,
    orbital_sems,
):
    n_pairs = 8
    wide = 2 * LANES
    groups = orbital_sems.shape[1]
    span = EDGE * EDGE // groups

    small = [
        pltpu.make_async_copy(src, dst, sems.at[i])
        for i, (src, dst) in enumerate(
            [
                (pairs_hbm, pairs),
                (x_factors_hbm, x_factors),
                (wave_hbm, wave),
                (valence_energy_hbm, valence_energy),
                (conduction_energy_hbm, conduction_energy),
                (z_factors_hbm, z_factors),
                (y_factors_hbm, y_factors),
            ]
        )
    ]
    for copy in small:
        copy.start()
    orbitals = []
    for n in range(groups):
        at = pl.ds(n * span, span)
        orbitals.append(
            [
                pltpu.make_async_copy(valence_hbm.at[:, :, at], valence.at[:, :, at], orbital_sems.at[0, n]),
                pltpu.make_async_copy(conduction_hbm.at[:, :, at], conduction.at[:, :, at], orbital_sems.at[1, n]),
            ]
        )
        for copy in orbitals[-1]:
            copy.start()
    for copy in small:
        copy.wait()

    a, b, c, _ = half_space(wave[...])
    rows_vector[...] = (a * 8 + (b >> 3)) * EDGE + c
    to_scalar = pltpu.make_async_copy(rows_vector, rows, sems.at[0])
    to_scalar.start()

    v_local = [lax.rem(pairs[0, p], valence.shape[0]) for p in range(n_pairs)]
    c_local = [lax.rem(pairs[1, p], conduction.shape[0]) for p in range(n_pairs)]
    sublane = lax.broadcasted_iota(jnp.int32, (8, LANES), 0)
    gap = jnp.ones((8, LANES), F32)
    for p in range(n_pairs):
        gap = jnp.where(sublane == p, conduction_energy[c_local[p]] - valence_energy[v_local[p]], gap)
    w = -4.0 / (total_pairs * gap)

    def x_stage(chunk, carry):
        lanes = pl.ds(pl.multiple_of(chunk * wide, wide), wide)
        for p in range(n_pairs):
            product = valence[v_local[p], :, lanes] * conduction[c_local[p], :, lanes]
            high, low = split(product)
            spectrum = jnp.dot(
                x_factors[...],
                jnp.concatenate([high, low], axis=0),
                preferred_element_type=F32,
            )
            spectrum = spectrum[:EDGE] + spectrum[EDGE:]
            for h in range(2):
                staged[2 * chunk + h, pl.ds(p, EDGE, stride=8), :] = spectrum[:, h * LANES : (h + 1) * LANES]
        return carry

    for n in range(groups):
        for copy in orbitals[n]:
            copy.wait()
        lax.fori_loop(n * span // wide, (n + 1) * span // wide, x_stage, 0, unroll=4)

    first = lax.broadcasted_iota(jnp.int32, (8, LANES), 1) < EDGE

    lower_lanes = lax.broadcasted_iota(jnp.int32, (EDGE, LANES), 1) < EDGE

    def yz_stage(a, carry):
        complex_plane = jnp.where((a & (HALF - 1)) == 0, 0.0, 1.0)
        at_re = pl.ds(pl.multiple_of(a * 8, 8), 8)
        at_im = pl.ds(pl.multiple_of(((a & (HALF - 1)) + HALF) * 8, 8), 8)
        re = [staged[y, at_re, :] for y in range(HALF)]
        im = [staged[y, at_im, :] * complex_plane for y in range(HALF)]
        re, im = small_dft(re, im)
        lower, upper = [], []
        for b in range(HALF):
            r, i = re[b], im[b]
            if b:
                c = y_factors[pl.ds(b, 8, stride=0), :]
                s = y_factors[pl.ds(b + HALF, 8, stride=0), :]
                r, i = r * c - i * s, r * s + i * c
            even = jnp.where(first, r, pltpu.roll(i, EDGE, 1))
            odd = jnp.where(first, pltpu.roll(r, EDGE, 1), i)
            lower.append(even + odd)
            upper.append(even - odd)
        high, low = split(jnp.concatenate(lower + upper, axis=0))
        out = lax.dot_general(
            z_factors[...],
            jnp.concatenate([high, low], axis=1),
            (((1,), (1,)), ((), ())),
            preferred_element_type=F32,
        )
        out = out[: 2 * EDGE] + out[2 * EDGE :]
        for n in range(4):
            re, im = out[:EDGE, n * LANES : (n + 1) * LANES], out[EDGE:, n * LANES : (n + 1) * LANES]
            at = pl.multiple_of((a * 8 + 2 * n) * EDGE, EDGE)
            table[pl.ds(at, EDGE), :] = jnp.where(lower_lanes, re, pltpu.roll(im, EDGE, 1))
            table[pl.ds(at + EDGE, EDGE), :] = jnp.where(lower_lanes, pltpu.roll(re, EDGE, 1), im)
        return carry

    lax.fori_loop(0, HALF + 1, yz_stage, 0, unroll=3)

    to_scalar.wait()
    per_row, per_col = left.shape[2] // LANES, right.shape[2] // LANES

    sublane_bits = [(sublane & (1 << i)) != 0 for i in range(3)]

    def pick(q, picked):
        line = rows.at[q]
        for j in range(0, LANES, 8):
            some = [table[pl.ds(line[j + t], 8, stride=0), :] for t in range(8)]
            for bit in sublane_bits:
                some = [jnp.where(bit, some[n + 1], some[n]) for n in range(0, len(some), 2)]
            picked[pl.ds(j, 8), :] = some[0]

    def finish(q, picked):
        turned = picked[...].T
        _, b, _, mirrored = half_space(wave[pl.ds(q, 8, stride=0), :])
        bits = [(b & (1 << i)) != 0 for i in range(3)]
        parts = []
        for k in range(2):
            some = [turned[k * EDGE + n * 8 : k * EDGE + n * 8 + 8] for n in range(8)]
            for bit in bits:
                some = [jnp.where(bit, some[n + 1], some[n]) for n in range(0, len(some), 2)]
            parts.append(some[0])
        re, im = parts
        im = jnp.where(mirrored, -im, im)
        plain = jnp.concatenate([re, im], axis=0).astype(BF)
        scaled = jnp.concatenate([w * re, w * im], axis=0).astype(BF)
        at = pl.multiple_of((q % per_row) * LANES, LANES)
        left[q // per_row, :, pl.ds(at, LANES)] = scaled
        at = pl.multiple_of((q % per_col) * LANES, LANES)
        right[q // per_col, :, pl.ds(at, LANES)] = plain

    count = wave.shape[0]
    pick(0, picked_0)

    def select(i, carry):
        pick(2 * i + 1, picked_1)
        finish(2 * i, picked_0)
        pick(jnp.minimum(2 * i + 2, count - 1), picked_0)
        finish(2 * i + 1, picked_1)
        return carry

    lax.fori_loop(0, count // 2, select, 0, unroll=8)


def densities(n_row, n_col, valence, conduction, valence_energy, conduction_energy, pair_list, sphere_index):
    n_pairs, waves = pair_list.shape[0], sphere_index.shape[0]
    tables = [jnp.asarray(x_table()), jnp.asarray(z_table()), jnp.asarray(y_table())]
    hbm = pl.BlockSpec(memory_space=pltpu.HBM)
    vmem = pl.BlockSpec(memory_space=pltpu.VMEM)
    return pl.pallas_call(
        lambda *refs: density_kernel(n_pairs * n_row * n_col, *refs),
        in_specs=[hbm] * 9,
        out_specs=[vmem, vmem],
        out_shape=[
            jax.ShapeDtypeStruct((n_row, 2 * n_pairs, waves // n_row), BF),
            jax.ShapeDtypeStruct((n_col, 2 * n_pairs, waves // n_col), BF),
        ],
        scratch_shapes=[
            pltpu.VMEM((HALF, n_pairs * EDGE, LANES), F32),
            pltpu.VMEM(((HALF + 1) * 8 * EDGE, LANES), F32),
            pltpu.VMEM(valence.shape, F32),
            pltpu.VMEM(conduction.shape, F32),
            pltpu.SMEM(valence_energy.shape, F32),
            pltpu.SMEM(conduction_energy.shape, F32),
            pltpu.SMEM((2, n_pairs), jnp.int32),
            pltpu.VMEM((waves // LANES, LANES), jnp.int32),
            pltpu.VMEM((waves // LANES, LANES), jnp.int32),
            pltpu.SMEM((waves // LANES, LANES), jnp.int32),
            pltpu.VMEM(tables[0].shape, BF),
            pltpu.VMEM(tables[1].shape, BF),
            pltpu.VMEM(tables[2].shape, F32),
            pltpu.VMEM((LANES, LANES), F32),
            pltpu.VMEM((LANES, LANES), F32),
            pltpu.SemaphoreType.DMA((7,)),
            pltpu.SemaphoreType.DMA((2, 4)),
        ],
        compiler_params=pltpu.CompilerParams(vmem_limit_bytes=60 * 1024 * 1024),
        name="density",
    )(
        valence,
        conduction,
        valence_energy,
        conduction_energy,
        pair_list.T,
        sphere_index.reshape(-1, LANES),
        *tables,
    )


def product_kernel(n_left, n_right, *refs):
    left, right, out = refs[:n_left], refs[n_left : n_left + n_right], refs[n_left + n_right]
    col, row = lax.axis_index("col"), lax.axis_index("row")
    left_slots, right_slots = left_places(col), right_places(row, col & 1)
    rows = out.shape[0]
    at = pl.multiple_of(pl.program_id(0) * rows, rows)
    out[...] = lax.dot_general(
        jnp.concatenate([piece[slot, :, pl.ds(at, rows)] for slot in right_slots for piece in left], axis=0),
        jnp.concatenate([piece[slot] for piece in right for slot in left_slots], axis=0),
        (((0,), (0,)), ((), ())),
        preferred_element_type=F32,
    )


def product(left, right):
    n_left, n_right = len(left), len(right)
    rows, cols = left[0].shape[2], right[0].shape[2]
    block = 512
    return pl.pallas_call(
        lambda *refs: product_kernel(n_left, n_right, *refs),
        grid=(rows // block,),
        in_specs=[pl.BlockSpec(memory_space=pltpu.VMEM)] * (n_left + n_right),
        out_specs=pl.BlockSpec((block, cols), lambda m: (m, 0)),
        out_shape=jax.ShapeDtypeStruct((rows, cols), F32),
        compiler_params=pltpu.CompilerParams(vmem_limit_bytes=32 * 1024 * 1024),
        name="product",
    )(*left, *right)


RING = 4


def shift(value, axis, stride, way):
    n_col, n_row = lax.axis_size("col"), lax.axis_size("row")

    def moved(i, step):
        place = i // stride % RING
        return i + ((place + step) % RING - place) * stride

    pairs = []
    for col in range(n_col):
        for row in range(n_row):
            step = way if col % 2 == 0 else -way
            to = (moved(col, step), row) if axis == "col" else (col, moved(row, step))
            pairs.append((col * n_row + row, to[0] * n_row + to[1]))
    return lax.ppermute(value, ("col", "row"), pairs)


def swap(value, axis, bit):
    count = lax.axis_size(axis)
    return lax.ppermute(value, axis, [(i, i ^ bit) for i in range(count)])


def ring_places(index, stride, core):
    place = lax.rem(lax.div(index, stride), RING)
    base = index - place * stride
    way = 1 - 2 * core
    return [base + lax.rem(place + step, RING) * stride for step in (0, RING - way, RING + way, 2)]


def right_places(row, core):
    return ring_places(row, 1, core) + ring_places(row ^ RING, 1, core)


def left_places(col):
    core = col & 1
    mine = ring_places(col, RING, core) + ring_places(col ^ 2, RING, core)
    theirs = ring_places(col ^ 1, RING, 1 - core) + ring_places(col ^ 3, RING, 1 - core)
    return mine + theirs


def per_device(valence, conduction, valence_energy, conduction_energy, pair_list, sphere_index):
    n_row, n_col = lax.axis_size("row"), lax.axis_size("col")
    left, right = densities(
        n_row, n_col, valence, conduction, valence_energy, conduction_energy, pair_list, sphere_index
    )
    right = lax.all_to_all(right, "col", split_axis=0, concat_axis=0, tiled=True)
    right, left = lax.optimization_barrier((right, left))
    left = lax.all_to_all(left, "row", split_axis=0, concat_axis=0, tiled=True)
    right_z = swap(right, "row", RING)
    rights = [right, shift(right, "row", 1, 1), shift(right, "row", 1, -1)]
    left_z = swap(left, "col", 2)
    lefts = [left, shift(left, "col", RING, 1), shift(left, "col", RING, -1)]
    rights += [shift(rights[1], "row", 1, 1), right_z, shift(right_z, "row", 1, 1), shift(right_z, "row", 1, -1)]
    lefts += [shift(lefts[1], "col", RING, 1)]
    lefts += [left_z, shift(left_z, "col", RING, 1), shift(left_z, "col", RING, -1), swap(lefts[3], "col", 2)]
    rights += [shift(rights[5], "row", 1, 1)]
    lefts += [swap(piece, "col", 1) for piece in lefts]
    return product(lefts, rights)


def solution(mesh):
    return jax.shard_map(
        per_device,
        mesh=mesh,
        in_specs=(
            P("row", None, None),
            P("col", None, None),
            P("row"),
            P("col"),
            P(("col", "row"), None),
            P(),
        ),
        out_specs=P("row", "col"),
        check_vma=False,
    )
```
